128 devices in a mesh: slab: 4 (over y), brick: 32 (over z, x, core).
Axes of the slice: x: 4, y: 4, z: 4, core: 2. Of those that a mesh axis runs over, the one named last changes fastest.
Arguments:
- verts: float32 [131072, 3, 128], P(('slab', 'brick')), may hold values from -4.2 to 4.2
- stiffness: float32 [131072, 128], P(('slab', 'brick')), may hold values from 0.2 to 2
- local_pairs: int32 [128, 2, 256], P(('slab', 'brick')), may hold values from 0 to 1023, as said below
- border_pick: int32 [128, 128], P(('slab', 'brick')), may hold values from 0 to 1023
- recv_src: int32 [128, 32, 8], P(('slab', 'brick')), may hold values from 0 to 127
- recv_pair: int32 [128, 32, 8], P(('slab', 'brick')), may hold values from -1 to 1023, as said below
- face_pick: int32 [128, 2, 64], P(('slab', 'brick')), may hold values from 0 to 1023
- face_pair: int32 [128, 2, 64], P(('slab', 'brick')), may hold values from -1 to 1023, as said below
Outputs:
- membrane_force: float32 [131072, 3, 128], P(('slab', 'brick'))
The draws below stay inside these ranges and needn't reach their ends.
Inputs may be any that keep to these rules, and one draw needn't show every extreme that they name: `local_pairs`: the two rows of a pair name different patches. `recv_pair`: -1 marks an empty slot; the slots for a device's own brick are empty. `face_pair`: -1 marks an empty slot.
All inputs are finite; a program needn't handle non-finite values.
Results may differ from the reference program's by a relative error of at most 0.0001.
Values sent between devices are 32-bit elements; how exact they have to be, the bound alone decides.
A program may use at most 128 MiB of HBM per device.

```python
import math
import jax
import jax.numpy as jnp
from jax import lax

NV = 128
PD = 1024
S = 8
B = 128
F = 64
LP = 256
NPATCH = 131072
N_SLAB = 4
N_BRICK = 32
DEVICES = 128


def draw_local_pairs(key, part):
    key_one, key_two = jax.random.split(jax.random.fold_in(key, 11))
    pushed_side = jax.random.randint(key_one, (DEVICES, 1, LP), 0, PD, dtype=jnp.int32)
    offsets = jax.random.randint(key_two, (DEVICES, 1, LP), 1, PD, dtype=jnp.int32)
    pushing_side = (pushed_side + offsets) % PD
    return jnp.concatenate([pushed_side, pushing_side], axis=1)


def busy_slots(key, shape):
    key_one, key_two, key_three = jax.random.split(key, 3)
    levels = jnp.array([1, 2, 4, 8], dtype=jnp.int32)
    level = levels[jax.random.randint(key_one, (shape[0], 1, 1), 0, 4, dtype=jnp.int32)]
    taken = jax.random.randint(key_two, shape, 0, 8, dtype=jnp.int32) < level
    values = jax.random.randint(key_three, shape, 0, PD, dtype=jnp.int32)
    return jnp.where(taken, values, -1)


def draw_recv_pair(key, part):
    slots = busy_slots(jax.random.fold_in(key, 23), (DEVICES, N_BRICK, S))
    own_brick = jnp.arange(DEVICES, dtype=jnp.int32) % N_BRICK
    same = own_brick[:, None, None] == jnp.arange(N_BRICK, dtype=jnp.int32)[None, :, None]
    return jnp.where(same, -1, slots)


def draw_face_pair(key, part):
    return busy_slots(jax.random.fold_in(key, 37), (DEVICES, 2, F))


def plant(values, own_key, least, top_value):
    shape = values.shape
    place = [jax.random.randint(jax.random.fold_in(own_key, axis), (), 0, shape[axis]) for axis in range(len(shape))]
    values = values.at[tuple(place)].set(least)
    longest = shape.index(max(shape))
    place[longest] = (place[longest] + 1) % shape[longest]
    return values.at[tuple(place)].set(top_value)


def block_levels(rng, dims, cuts, smallest, high):
    loudness, own = 1.0, jax.random.fold_in(rng, 6)
    for dim, blocks in cuts:
        draws = jnp.exp(jax.random.uniform(jax.random.fold_in(own, dim), (blocks,), jnp.float32, smallest / len(cuts), high / len(cuts)))
        loudness = loudness * jnp.repeat(draws, dims[dim] // blocks).reshape([-1 if axis == dim else 1 for axis in range(len(dims))])
    return loudness


def bell_draw(rng, extent, spread, most, cuts=(), held_as=jnp.bfloat16):
    level = block_levels(rng, extent, cuts, -0.22, 0.18) if cuts else 1.0
    values = jax.random.normal(rng, extent, jnp.float32) * spread * level
    return jnp.minimum(jnp.maximum(values, -most), most).astype(held_as)


def setup_inputs(seed: int = 0) -> dict:
    seeds = jax.random.split(jax.random.key(seed), 9)
    return {
        "verts": bell_draw(seeds[0], (NPATCH, 3, NV), 0.7, 4.2, ((0, 128),), jnp.float32),
        "stiffness": jnp.clip(jnp.exp(math.log(2.0) - 2.3025851 * jax.random.uniform(seeds[1], (NPATCH, NV), jnp.float32) ** block_levels(seeds[1], (NPATCH, NV), ((0, 128),), -0.2, 0.2)), 0.2, 2.0),
        "local_pairs": draw_local_pairs(jax.random.fold_in(seeds[8], 71), 0),
        "border_pick": plant(jax.random.randint(seeds[3], (DEVICES, B), 0, PD), jax.random.fold_in(seeds[3], 1), 0, PD - 1).astype(jnp.int32),
        "recv_src": plant(jax.random.randint(seeds[4], (DEVICES, N_BRICK, S), 0, B), jax.random.fold_in(seeds[4], 1), 0, B - 1).astype(jnp.int32),
        "recv_pair": draw_recv_pair(jax.random.fold_in(seeds[8], 71), 0),
        "face_pick": plant(jax.random.randint(seeds[6], (DEVICES, 2, F), 0, PD), jax.random.fold_in(seeds[6], 1), 0, PD - 1).astype(jnp.int32),
        "face_pair": draw_face_pair(jax.random.fold_in(seeds[8], 71), 0),
    }


highest = lax.Precision.HIGHEST


def centroids(points):
    return (points + jnp.roll(points, -1, axis=-1) + jnp.roll(points, -2, axis=-1)) / 3.0


def tile_forces(own_points, far_centres, far_weight):
    own_sq = jnp.sum(own_points * own_points, axis=1)
    far_sq = jnp.sum(far_centres * far_centres, axis=1)
    cross_dot = jnp.einsum("pci,pcj->pij", own_points, far_centres, precision=highest)
    dist_sq = own_sq[:, :, None] + far_sq[:, None, :] - 2.0 * cross_dot
    energy = far_weight[:, None, :] * jnp.exp(-0.5 * dist_sq) / own_points.shape[-1]
    row_total = jnp.sum(energy, axis=2)
    col_total = jnp.sum(energy, axis=1)
    pushed = own_points * row_total[:, None, :] - jnp.einsum("pcj,pij->pci", far_centres, energy, precision=highest)
    reaction = far_centres * col_total[:, None, :] - jnp.einsum("pci,pij->pcj", own_points, energy, precision=highest)
    return pushed, reaction


def spread_triangles(pushed, reaction):
    return pushed + (reaction + jnp.roll(reaction, 1, axis=-1) + jnp.roll(reaction, 2, axis=-1)) / 3.0


def reference(verts, stiffness, local_pairs, border_pick, recv_src, recv_pair, face_pick, face_pair):
    device = jnp.arange(DEVICES, dtype=jnp.int32)
    slab_of = device // N_BRICK
    offset = device * PD
    target_loc = (offset[:, None] + local_pairs[:, 0, :]).reshape(-1)
    anchor_loc = (offset[:, None] + local_pairs[:, 1, :]).reshape(-1)
    usable_loc = jnp.ones(target_loc.shape, dtype=verts.dtype)
    source = slab_of[:, None] * N_BRICK + jnp.arange(N_BRICK, dtype=jnp.int32)[None, :]
    anchor_brk = (source[:, :, None] * PD + border_pick[source[:, :, None], recv_src]).reshape(-1)
    target_brk = (offset[:, None, None] + jnp.maximum(recv_pair, 0)).reshape(-1)
    usable_brk = (recv_pair >= 0).astype(verts.dtype).reshape(-1)
    lower_dev = jnp.maximum(device - N_BRICK, 0)
    upper_dev = jnp.minimum(device + N_BRICK, DEVICES - 1)
    anchor_low = (lower_dev[:, None] * PD + face_pick[lower_dev, 1, :]).reshape(-1)
    anchor_up = (upper_dev[:, None] * PD + face_pick[upper_dev, 0, :]).reshape(-1)
    target_low = (offset[:, None] + jnp.maximum(face_pair[:, 0, :], 0)).reshape(-1)
    target_up = (offset[:, None] + jnp.maximum(face_pair[:, 1, :], 0)).reshape(-1)
    usable_low = ((slab_of > 0)[:, None] & (face_pair[:, 0, :] >= 0)).astype(verts.dtype).reshape(-1)
    usable_up = ((slab_of < N_SLAB - 1)[:, None] & (face_pair[:, 1, :] >= 0)).astype(verts.dtype).reshape(-1)
    targets = jnp.concatenate([target_loc, target_brk, target_low, target_up])
    anchors = jnp.concatenate([anchor_loc, anchor_brk, anchor_low, anchor_up])
    usable = jnp.concatenate([usable_loc, usable_brk, usable_low, usable_up])
    total = targets.shape[0]
    block_size = math.gcd(total, 256)
    centres = centroids(verts)

    def step(totals, pieces):
        push_acc, react_acc = totals
        target_idx, anchor_idx, usable_rows = pieces
        weight = stiffness[anchor_idx] * usable_rows[:, None]
        pushed, reaction = tile_forces(verts[target_idx], centres[anchor_idx], weight)
        return (push_acc.at[target_idx].add(pushed), react_acc.at[anchor_idx].add(reaction)), None

    start = (jnp.zeros_like(verts), jnp.zeros_like(verts))
    pieces = (targets.reshape(-1, block_size), anchors.reshape(-1, block_size), usable.reshape(-1, block_size))
    (push_acc, react_acc), ignored = lax.scan(step, start, pieces)
    return spread_triangles(push_acc, react_acc)
```

```python
import math

import jax
import jax.numpy as jnp
from jax import lax
from jax.experimental import pallas as pl
from jax.experimental.pallas import tpu as pltpu
from jax.sharding import PartitionSpec as P

f32 = jnp.float32
bf16 = jnp.bfloat16
i32 = jnp.int32
MESH = pl.DeviceIdType.MESH

NP = 1024
NV = 128
NB = 32
NS = 8
NF = 64
NR = NB * NS + 2 * NF
NL = 256
SQ = math.sqrt(math.log2(math.e))
FAR = 1.0e4
U = 4
DN = (((1,), (1,)), ((), ()))

vm = pl.BlockSpec(memory_space=pltpu.VMEM)
sm = pl.BlockSpec(memory_space=pltpu.SMEM)


def greet(me_t, me_b):
    sem = pltpu.get_barrier_semaphore()

    def one(o, c):
        pl.semaphore_signal(
            sem, inc=1, device_id=(me_t, lax.rem(me_b + o, NB)), device_id_type=MESH
        )
        return c

    lax.fori_loop(1, NB, one, 0)

    @pl.when(me_t > 0)
    def _():
        pl.semaphore_signal(sem, inc=1, device_id=(me_t - 1, me_b), device_id_type=MESH)

    @pl.when(me_t < 3)
    def _():
        pl.semaphore_signal(sem, inc=1, device_id=(me_t + 1, me_b), device_id_type=MESH)

    return sem


def greeted(sem, me_t):
    faces = (me_t > 0).astype(i32) + (me_t < 3).astype(i32)
    pl.semaphore_wait(sem, NB - 1 + faces)


def brick_copy(src, dst, s_sem, r_sem, me_t, me_b, o):
    peer = lax.rem(me_b + o, NB)
    return pltpu.make_async_remote_copy(
        src_ref=src.at[peer],
        dst_ref=dst.at[me_b],
        send_sem=s_sem.at[peer],
        recv_sem=r_sem.at[me_b],
        device_id=(me_t, peer),
        device_id_type=MESH,
    )


def brick_arrival(src, dst, s_sem, r_sem, me_t, me_b, o):
    peer = lax.rem(me_b + o, NB)
    return pltpu.make_async_remote_copy(
        src_ref=src.at[peer],
        dst_ref=dst.at[peer],
        send_sem=s_sem.at[peer],
        recv_sem=r_sem.at[peer],
        device_id=(me_t, peer),
        device_id_type=MESH,
    )


def face_copy(src, dst, s_sem, r_sem, me_t, me_b, side):
    step = -1 if side == 0 else 1
    return pltpu.make_async_remote_copy(
        src_ref=src.at[side],
        dst_ref=dst.at[1 - side],
        send_sem=s_sem.at[side],
        recv_sem=r_sem.at[1 - side],
        device_id=(me_t + step, me_b),
        device_id_type=MESH,
    )


def face_arrival(src, dst, s_sem, r_sem, me_t, me_b, side):
    step = -1 if side == 0 else 1
    return pltpu.make_async_remote_copy(
        src_ref=src.at[side],
        dst_ref=dst.at[side],
        send_sem=s_sem.at[side],
        recv_sem=r_sem.at[side],
        device_id=(me_t + step, me_b),
        device_id_type=MESH,
    )


def finish(src_b, dst_b, src_f, dst_f, sb, rb, sf, rf, me_t, me_b):
    def one(o, c):
        brick_arrival(src_b, dst_b, sb, rb, me_t, me_b, o).wait_recv()
        brick_copy(src_b, dst_b, sb, rb, me_t, me_b, o).wait_send()
        return c

    lax.fori_loop(1, NB, one, 0)
    for side in range(2):

        @pl.when((me_t > 0) if side == 0 else (me_t < 3))
        def _(side=side):
            face_arrival(src_f, dst_f, sf, rf, me_t, me_b, side).wait_recv()
            face_copy(src_f, dst_f, sf, rf, me_t, me_b, side).wait_send()


def ask_kernel(rp, rs, fp, verts, got_b, got_f, out_b, out_f, sb, rb, sf, rf):
    me_t = lax.axis_index("slab")
    me_b = lax.axis_index("brick")
    sem = greet(me_t, me_b)

    def row(idx):
        return jnp.where(idx >= 0, verts[jnp.maximum(idx, 0)], FAR)

    def fill_face(k, c):
        for side in range(2):
            idx = fp[side, k]
            out_f[side, k, 0:3] = row(idx)
            out_f[side, k, 3:4] = jnp.full((1, NV), jnp.minimum(idx, 0).astype(f32))
        return c

    lax.fori_loop(0, NF, fill_face, 0)
    none = jnp.full((NS, 1, NV), -1.0, f32)
    got_b[me_b, :, 0:3, :] = jnp.full((NS, 3, NV), FAR, f32)
    got_b[me_b, :, 3:4, :] = none

    @pl.when(me_t == 0)
    def _():
        got_f[0] = jnp.full((NF, 4, NV), -1.0, f32)

    @pl.when(me_t == 3)
    def _():
        got_f[1] = jnp.full((NF, 4, NV), -1.0, f32)

    greeted(sem, me_t)
    for side in range(2):

        @pl.when((me_t > 0) if side == 0 else (me_t < 3))
        def _(side=side):
            face_copy(out_f, got_f, sf, rf, me_t, me_b, side).start()

    def send(o, c):
        s = lax.rem(me_b + o, NB)
        for k in range(NS):
            idx = rp[s, k]
            out_b[s, k, 0:3] = row(idx)
            src = jnp.where(idx >= 0, rs[s, k], -1)
            out_b[s, k, 3:4] = jnp.full((1, NV), src.astype(f32))
        brick_copy(out_b, got_b, sb, rb, me_t, me_b, o).start()
        return c

    lax.fori_loop(1, NB, send, 0)
    finish(out_b, got_b, out_f, got_f, sb, rb, sf, rf, me_t, me_b)


def ask(rp, rs, fp, verts):
    return pl.pallas_call(
        ask_kernel,
        name="ask",
        out_shape=(
            jax.ShapeDtypeStruct((NB, NS, 4, NV), f32),
            jax.ShapeDtypeStruct((2, NF, 4, NV), f32),
        ),
        in_specs=[sm, sm, sm, vm],
        out_specs=(vm, vm),
        scratch_shapes=[
            pltpu.VMEM((NB, NS, 4, NV), f32),
            pltpu.VMEM((2, NF, 4, NV), f32),
            pltpu.SemaphoreType.DMA((NB,)),
            pltpu.SemaphoreType.DMA((NB,)),
            pltpu.SemaphoreType.DMA((2,)),
            pltpu.SemaphoreType.DMA((2,)),
        ],
        compiler_params=pltpu.CompilerParams(collective_id=0, has_side_effects=True),
    )(rp, rs, fp, verts)


def give_kernel(out_b, out_f, got_b, got_f, sb, rb, sf, rf):
    me_t = lax.axis_index("slab")
    me_b = lax.axis_index("brick")
    sem = greet(me_t, me_b)
    got_b[me_b] = jnp.zeros((NS, 3, NV), f32)

    @pl.when(me_t == 0)
    def _():
        got_f[0] = jnp.zeros((NF, 3, NV), f32)

    @pl.when(me_t == 3)
    def _():
        got_f[1] = jnp.zeros((NF, 3, NV), f32)

    greeted(sem, me_t)
    for side in range(2):

        @pl.when((me_t > 0) if side == 0 else (me_t < 3))
        def _(side=side):
            face_copy(out_f, got_f, sf, rf, me_t, me_b, side).start()

    def send(o, c):
        brick_copy(out_b, got_b, sb, rb, me_t, me_b, o).start()
        return c

    lax.fori_loop(1, NB, send, 0)
    finish(out_b, got_b, out_f, got_f, sb, rb, sf, rf, me_t, me_b)


def give(out_b, out_f):
    return pl.pallas_call(
        give_kernel,
        name="give",
        out_shape=(
            jax.ShapeDtypeStruct((NB, NS, 3, NV), f32),
            jax.ShapeDtypeStruct((2, NF, 3, NV), f32),
        ),
        in_specs=[vm, vm],
        out_specs=(vm, vm),
        scratch_shapes=[
            pltpu.SemaphoreType.DMA((NB,)),
            pltpu.SemaphoreType.DMA((NB,)),
            pltpu.SemaphoreType.DMA((2,)),
            pltpu.SemaphoreType.DMA((2,)),
        ],
        compiler_params=pltpu.CompilerParams(collective_id=1, has_side_effects=True),
    )(out_b, out_f)


def split(x):
    high = x.astype(bf16).astype(f32)
    return high, x - high


def ahead(v, k):
    return pltpu.roll(v, NV - k, 1)


def energies(xs, vs, stiff, e_ij, e_ji):
    one = jnp.ones((8, NV), f32)
    zero = jnp.zeros((8, NV), f32)
    cs = [(v + ahead(v, 1) + ahead(v, 2)) * (1.0 / 3.0) for v in vs]
    xp = [x * SQ for x in xs]
    cp = [c * SQ for c in cs]
    x1, x2 = zip(*[split(x) for x in xp])
    c1, c2 = zip(*[split(c) for c in cp])
    n = -0.5 * (xp[0] * xp[0] + xp[1] * xp[1] + xp[2] * xp[2])
    m = -0.5 * (cp[0] * cp[0] + cp[1] * cp[1] + cp[2] * cp[2]) + jnp.log2(stiff) - 7.0
    n1, r = split(n)
    n2, n3 = split(r)
    m1, r = split(m)
    m2, m3 = split(r)
    a = jnp.concatenate([*x1, *x1, *x2, n1, n2, n3, one, one, one, zero], 0).astype(bf16)
    b = jnp.concatenate([*c1, *c2, *c1, one, one, one, m1, m2, m3, zero], 0).astype(bf16)
    at = a.T
    lx = jnp.concatenate([*x1, *x2, one, zero], 0).astype(bf16)
    lc = jnp.concatenate([*c1, *c2, one, zero], 0).astype(bf16)
    sub = lax.broadcasted_iota(i32, (NV, NV), 0) % 8
    for q in range(0, 8, 2):
        bq = jnp.concatenate([jnp.where(sub == q + k, b, jnp.zeros_like(b)) for k in range(2)], 1)
        e = jnp.exp2(jnp.dot(at, bq, preferred_element_type=f32))
        eh = e.astype(bf16)
        el = (e - eh.astype(f32)).astype(bf16)
        e_ij[0:NV, q * NV : (q + 2) * NV] = eh
        e_ij[NV : 2 * NV, q * NV : (q + 2) * NV] = el
        for k in range(2):
            o = (q + k) * NV
            e_ji[o : o + NV, 0:NV] = eh[:, k * NV : (k + 1) * NV]
            e_ji[o : o + NV, NV : 2 * NV] = el[:, k * NV : (k + 1) * NV]
    return xs, cs, lx, lc


def diagonal(r):
    sub = lax.broadcasted_iota(i32, (8, NV), 0)
    out = []
    for k in range(7):
        o = r[8 * k : 8 * k + 8, 0:NV]
        for q in range(1, 8):
            o = jnp.where(sub == q, r[8 * k : 8 * k + 8, q * NV : (q + 1) * NV], o)
        out.append(o)
    return out


def forces(xs, cs, lx, lc, e_ij, e_ji):
    rx = diagonal(jnp.dot(jnp.concatenate([lx, lx], 1), e_ij[...], preferred_element_type=f32))
    rc = diagonal(
        lax.dot_general(
            jnp.concatenate([lc, lc], 1), e_ji[...], DN, preferred_element_type=f32
        )
    )
    inv = 1.0 / SQ
    react = [cs[k] * rx[6] - (rx[k] + rx[3 + k]) * inv for k in range(3)]
    push = [xs[k] * rc[6] - (rc[k] + rc[3 + k]) * inv for k in range(3)]
    return push, react


def pair_kernel(
    loc, pick, fpick, src, verts, stiff, got_b, got_f,
    acc_p, acc_r, back_b, back_f,
    order, xg, vg, sg, pg, rg, e_ij, e_ji, far, back,
):
    def clear(i, c):
        acc_p[pl.ds(i * 16, 16)] = jnp.zeros((16, 3, NV), f32)
        acc_r[pl.ds(i * 16, 16)] = jnp.zeros((16, 3, NV), f32)
        return c

    lax.fori_loop(0, NP // 16, clear, 0)

    def load(i, c):
        far[pl.ds(i * NS, NS)] = got_b[i]
        return c

    lax.fori_loop(0, NB, load, 0)
    for side in range(2):
        far[pl.ds(NB * NS + side * NF, NF)] = got_f[side]
    far[NR] = jnp.full((4, NV), FAR, f32)

    def count(i, n):
        order[n] = i
        return n + (src[i] >= 0).astype(i32)

    n = lax.fori_loop(0, NR, count, jnp.int32(0))

    def pad(i, c):
        order[n + i] = NR
        return c

    lax.fori_loop(0, 8 * U, pad, 0)

    def block(get_x, get_b, put):
        kept = []

        def last(u):
            push, react = forces(*kept[u], e_ij.at[u], e_ji.at[u])
            for c in range(3):
                pg[u, :, c, :] = push[c]
                rg[u, :, c, :] = react[c]

        where = []
        for u in range(U):
            for p in range(8):
                x = get_x(u * 8 + p)
                b = get_b(u * 8 + p)
                where.append(b)
                xg[u, p] = x
                vg[u, p] = verts[b]
                sg[u, pl.ds(p, 1), :] = stiff[pl.ds(b, 1), :]
        for u in range(U):
            xs = [xg[u, :, c, :] for c in range(3)]
            vs = [vg[u, :, c, :] for c in range(3)]
            kept.append(energies(xs, vs, sg[u], e_ij.at[u], e_ji.at[u]))
            if u > 0:
                last(u - 1)
        last(U - 1)
        for u in range(U):
            for p in range(8):
                put(u * 8 + p, pg[u, p])
                acc_r[where[u * 8 + p]] += rg[u, p]

    def local_step(g, c):
        base = g * 8 * U

        def put(i, v):
            acc_p[loc[0, base + i]] += v

        block(lambda i: verts[loc[0, base + i]], lambda i: loc[1, base + i], put)
        return c

    lax.fori_loop(0, NL // (8 * U), local_step, 0)

    def far_step(g, c):
        base = g * 8 * U

        def get_b(i):
            o = order[base + i]
            s = jnp.maximum(src[o], 0)
            brick = pick[jnp.minimum(s, NV - 1)]
            j = jnp.clip(o - NB * NS, 0, 2 * NF - 1)
            face = fpick[j]
            return jnp.where(o < NB * NS, brick, face)

        def put(i, v):
            back[order[base + i]] = v

        block(lambda i: far[order[base + i], 0:3], get_b, put)
        return c

    lax.fori_loop(0, (n + 8 * U - 1) // (8 * U), far_step, 0)

    def store(i, c):
        back_b[i] = back[pl.ds(i * NS, NS)]
        return c

    lax.fori_loop(0, NB, store, 0)
    for side in range(2):
        back_f[side] = back[pl.ds(NB * NS + side * NF, NF)]


def pairs(loc, pick, fpick, src, verts, stiff, got_b, got_f):
    acc = jax.ShapeDtypeStruct((NP, 3, NV), f32)
    return pl.pallas_call(
        pair_kernel,
        name="pairs",
        out_shape=(
            acc,
            acc,
            jax.ShapeDtypeStruct((NB, NS, 3, NV), f32),
            jax.ShapeDtypeStruct((2, NF, 3, NV), f32),
        ),
        in_specs=[sm] * 4 + [vm] * 4,
        out_specs=(vm,) * 4,
        scratch_shapes=[
            pltpu.SMEM((NR + 8 * U,), i32),
            pltpu.VMEM((U, 8, 3, NV), f32),
            pltpu.VMEM((U, 8, 3, NV), f32),
            pltpu.VMEM((U, 8, NV), f32),
            pltpu.VMEM((U, 8, 3, NV), f32),
            pltpu.VMEM((U, 8, 3, NV), f32),
            pltpu.VMEM((U, 2 * NV, 8 * NV), bf16),
            pltpu.VMEM((U, 8 * NV, 2 * NV), bf16),
            pltpu.VMEM((NR + 1, 4, NV), f32),
            pltpu.VMEM((NR + 1, 3, NV), f32),
        ],
        compiler_params=pltpu.CompilerParams(vmem_limit_bytes=48 << 20),
    )(loc, pick, fpick, src, verts, stiff, got_b, got_f)


def merge_kernel(rp, fp, acc_p, acc_r, got_b, got_f, out):
    def spread(i, c):
        for h in range(2):
            at = pl.ds(i * 16 + h * 8, 8)
            r = acc_r[at]
            s = r + pltpu.roll(r, 1, 2) + pltpu.roll(r, 2, 2)
            out[at] = acc_p[at] + s * (1.0 / 3.0)
        return c

    lax.fori_loop(0, NP // 16, spread, 0)

    def brick(s, c):
        for k in range(NS):
            idx = rp[s, k]

            @pl.when(idx >= 0)
            def _(k=k, idx=idx):
                out[idx] += got_b[s, k]

        return c

    lax.fori_loop(0, NB, brick, 0)
    me_t = lax.axis_index("slab")

    def face(k, c):
        for side in range(2):
            idx = fp[side, k]
            there = (me_t > 0) if side == 0 else (me_t < 3)

            @pl.when((idx >= 0) & there)
            def _(side=side, idx=idx):
                out[idx] += got_f[side, k]

        return c

    lax.fori_loop(0, NF, face, 0)


def merge(rp, fp, acc_p, acc_r, got_b, got_f):
    return pl.pallas_call(
        merge_kernel,
        name="merge",
        out_shape=jax.ShapeDtypeStruct((NP, 3, NV), f32),
        in_specs=[sm] * 2 + [vm] * 4,
        out_specs=vm,
        compiler_params=pltpu.CompilerParams(vmem_limit_bytes=48 << 20),
    )(rp, fp, acc_p, acc_r, got_b, got_f)


def body(verts, stiffness, local_pairs, border_pick, recv_src, recv_pair, face_pick, face_pair):
    rp = recv_pair[0]
    fp = face_pair[0]
    got_b, got_f = ask(rp, recv_src[0], fp, verts)
    src = jnp.concatenate([got_b[:, :, 3, 0].reshape(-1), got_f[:, :, 3, 0].reshape(-1)])
    acc_p, acc_r, back_b, back_f = pairs(
        local_pairs[0],
        border_pick[0],
        face_pick[0].reshape(-1),
        src.astype(i32),
        verts,
        stiffness,
        got_b,
        got_f,
    )
    ret_b, ret_f = give(back_b, back_f)
    return merge(rp, fp, acc_p, acc_r, ret_b, ret_f)


def solution(mesh):
    both = ("slab", "brick")
    placed = (
        P(both, None, None),
        P(both, None),
        P(both, None, None),
        P(both, None),
        P(both, None, None),
        P(both, None, None),
        P(both, None, None),
        P(both, None, None),
    )
    return jax.shard_map(
        body, mesh=mesh, in_specs=placed, out_specs=P(both, None, None), check_vma=False
    )
```

```python
import math

import jax
import jax.numpy as jnp
from jax import lax
from jax.experimental import pallas as pl
from jax.experimental.pallas import tpu as pltpu
from jax.sharding import PartitionSpec as P

f32 = jnp.float32
bf16 = jnp.bfloat16
i32 = jnp.int32
MESH = pl.DeviceIdType.MESH

NP = 1024
NV = 128
NB = 32
NS = 8
NF = 64
NBS = NB * NS
NL = 256
FIRST = 20
SQ = math.sqrt(math.log2(math.e))
FAR = 1.0e4
U = 4
LAG = 4
DN = (((1,), (1,)), ((), ()))
D0 = (((0,), (0,)), ((), ()))

vm = pl.BlockSpec(memory_space=pltpu.VMEM)
sm = pl.BlockSpec(memory_space=pltpu.SMEM)


def greet(me_t, me_b):
    sem = pltpu.get_barrier_semaphore()

    def one(o, c):
        pl.semaphore_signal(
            sem, inc=1, device_id=(me_t, lax.rem(me_b + o, NB)), device_id_type=MESH
        )
        return c

    lax.fori_loop(1, NB, one, 0)

    @pl.when(me_t > 0)
    def _():
        pl.semaphore_signal(sem, inc=1, device_id=(me_t - 1, me_b), device_id_type=MESH)

    @pl.when(me_t < 3)
    def _():
        pl.semaphore_signal(sem, inc=1, device_id=(me_t + 1, me_b), device_id_type=MESH)

    return sem


def greeted(sem, me_t):
    faces = (me_t > 0).astype(i32) + (me_t < 3).astype(i32)
    pl.semaphore_wait(sem, NB - 1 + faces)


class Brick:
    def __init__(self, src, dst, s_sem, r_sem, me_t, me_b):
        self.a = (src, dst, s_sem, r_sem, me_t, me_b)

    def copy(self, o, arrival=False):
        src, dst, s_sem, r_sem, me_t, me_b = self.a
        peer = lax.rem(me_b + o, NB)
        at = peer if arrival else me_b
        return pltpu.make_async_remote_copy(
            src_ref=src.at[peer],
            dst_ref=dst.at[at],
            send_sem=s_sem.at[peer],
            recv_sem=r_sem.at[at],
            device_id=(me_t, peer),
            device_id_type=MESH,
        )

    def start(self):
        def one(o, c):
            self.copy(o).start()
            return c

        lax.fori_loop(1, NB, one, 0)

    def wait(self):
        def one(o, c):
            self.copy(o, True).wait_recv()
            self.copy(o).wait_send()
            return c

        lax.fori_loop(1, NB, one, 0)


class Face:
    def __init__(self, src, dst, s_sem, r_sem, me_t, me_b):
        self.a = (src, dst, s_sem, r_sem, me_t, me_b)

    def copy(self, side, arrival=False):
        src, dst, s_sem, r_sem, me_t, me_b = self.a
        at = side if arrival else 1 - side
        return pltpu.make_async_remote_copy(
            src_ref=src.at[side],
            dst_ref=dst.at[at],
            send_sem=s_sem.at[side],
            recv_sem=r_sem.at[at],
            device_id=(me_t + (1 if side else -1), me_b),
            device_id_type=MESH,
        )

    def there(self, side):
        return (self.a[4] < 3) if side else (self.a[4] > 0)

    def start(self):
        for side in range(2):

            @pl.when(self.there(side))
            def _(side=side):
                self.copy(side).start()

    def wait(self):
        for side in range(2):

            @pl.when(self.there(side))
            def _(side=side):
                self.copy(side, True).wait_recv()
                self.copy(side).wait_send()


def split(x):
    high = x.astype(bf16).astype(f32)
    return high, x - high


def ahead(v, k):
    return pltpu.roll(v, NV - k, 1)


def prepare(xs, vs, stiff, lx, lc):
    one = jnp.ones((8, NV), f32)
    zero = jnp.zeros((8, NV), f32)
    cs = [(v + ahead(v, 1) + ahead(v, 2)) * (1.0 / 3.0) for v in vs]
    xp = [x * SQ for x in xs]
    cp = [c * SQ for c in cs]
    x1, x2 = zip(*[split(x) for x in xp])
    c1, c2 = zip(*[split(c) for c in cp])
    n = -0.5 * (xp[0] * xp[0] + xp[1] * xp[1] + xp[2] * xp[2])
    m = -0.5 * (cp[0] * cp[0] + cp[1] * cp[1] + cp[2] * cp[2]) + jnp.log2(stiff) - 7.0
    n1, r = split(n)
    n2, n3 = split(r)
    m1, r = split(m)
    m2, m3 = split(r)
    a = jnp.concatenate([*x1, *x1, *x2, n1, n2, n3, one, one, one, zero], 0).astype(bf16)
    b = jnp.concatenate([*c1, *c2, *c1, one, one, one, m1, m2, m3, zero], 0).astype(bf16)
    for ref, rows in ((lx, [*x1, *x2, one, zero]), (lc, [*c1, *c2, one, zero])):
        for k, r in enumerate(rows):
            ref[pl.ds(k, 8, stride=8), :] = r
    return cs, a.T, b


def energies(at, b, t):
    sub = lax.broadcasted_iota(i32, (NV, NV), 0) % 8
    zero = jnp.zeros_like(b)
    two = jnp.concatenate([jnp.where(sub == 2 * t + k, b, zero) for k in range(2)], 1)
    e = jnp.exp2(jnp.dot(at, two, preferred_element_type=f32))
    high = e.astype(bf16)
    return high, (e - high.astype(f32)).astype(bf16)


def sums(t, e, lx, lc, rx, rc):
    h0, l0, h1, l1 = e
    rows = slice(16 * t, 16 * t + 16)
    x = lx[rows, :].astype(bf16)
    c = lc[rows, :].astype(bf16)
    cat = jnp.concatenate
    e_ij = cat([cat([h0, h1], 1), cat([l0, l1], 1)], 0)
    e_ji = cat([cat([h0, l0], 1), cat([h1, l1], 1)], 0)
    r = jnp.dot(cat([x, x], 1), e_ij, preferred_element_type=f32)
    s = lax.dot_general(cat([c, c], 1), e_ji, DN, preferred_element_type=f32)
    for ref, v in ((rx, r), (rc, s)):
        ref[16 * t : 16 * t + 8, :] = v[0:8, 0:NV]
        ref[16 * t + 8 : 16 * t + 16, :] = v[8:16, NV : 2 * NV]


def forces(xs, cs, rx, rc):
    def get(ref, k):
        return ref[pl.ds(k, 8, stride=8), :]

    inv = 1.0 / SQ
    q = get(rx, 6)
    r = get(rc, 6)
    react = [cs[k] * q - (get(rx, k) + get(rx, 3 + k)) * inv for k in range(3)]
    push = [xs[k] * r - (get(rc, k) + get(rc, 3 + k)) * inv for k in range(3)]
    return push, react


class Groups:
    def __init__(self, xg, vg, sg, lx, lc, rx, rc, eb):
        self.r = (xg, vg, sg, lx, lc, rx, rc, eb)

    def run(self, first, count, load, put):
        xg, vg, sg, lx, lc, rx, rc, eb = self.r
        n = U * 4

        def second(i, g):
            u, t = divmod(i, 4)
            e = [eb[u, t, k] for k in range(4)]
            sums(t, e, lx.at[u], lc.at[u], rx.at[u], rc.at[u])
            if t == 3:
                xs = [xg[u, c] for c in range(3)]
                cs = [vg[u, c] for c in range(3)]
                put(g, *forces(xs, cs, rx.at[u], rc.at[u]))

        def step(s, carry):
            base = first + s * U
            for i in range(n):
                u, t = divmod(i, 4)
                if t == 0:
                    load(u, base + u)
                    xs = [xg[u, c] for c in range(3)]
                    cs, at, b = prepare(xs, [vg[u, c] for c in range(3)], sg[u], lx.at[u], lc.at[u])
                    for c in range(3):
                        vg[u, c] = cs[c]
                j = i - LAG
                ju = (j % n) // 4
                second(j % n, base + ju if j >= 0 else jnp.maximum(base + ju - U, first))
                high, low = energies(at, b, t)
                eb[u, t, 0] = high[:, :NV]
                eb[u, t, 1] = low[:, :NV]
                eb[u, t, 2] = high[:, NV:]
                eb[u, t, 3] = low[:, NV:]
            return carry

        lax.fori_loop(0, count // U, step, 0)
        for j in range(n - LAG, n):
            second(j, first + count - U + j // 4)


def rows8(g, base=0):
    return pl.ds(pl.multiple_of(base + g * 8, 8), 8)


def pair_kernel(
    rp, fp, loc, pick, fpick, rs, verts, stiff,
    push_l, react, ret_b, ret_f, meta,
    got_b, got_f, out_b, out_f, back_b, back_f, brd, gv,
    xg, vg, sg, lx, lc, rx, rc, eb, sems, fsems,
):
    me_t = lax.axis_index("slab")
    me_b = lax.axis_index("brick")
    barrier = greet(me_t, me_b)
    ask_b = Brick(out_b, got_b, sems.at[0], sems.at[1], me_t, me_b)
    ask_f = Face(out_f, got_f, fsems.at[0], fsems.at[1], me_t, me_b)
    give_b = Brick(back_b, ret_b, sems.at[2], sems.at[3], me_t, me_b)
    give_f = Face(back_f, ret_f, fsems.at[2], fsems.at[3], me_t, me_b)

    def row(c, idx):
        return jnp.where(idx >= 0, verts[c, pl.ds(jnp.maximum(idx, 0), 1), :], FAR)

    def fill_brick(s, carry):
        for k in range(NS):
            idx = rp[k, s]
            for c in range(3):
                out_b[s, c, k : k + 1, :] = row(c, idx)
        return carry

    lax.fori_loop(0, NB, fill_brick, 0)
    for s in range(NB):
        out_b[s, 3] = jnp.broadcast_to(rs[:, s : s + 1].astype(f32), (NS, NV))

    def fill_face(i, carry):
        for side in range(2):
            for k in range(8):
                idx = fp[side, i * 8 + k]
                for c in range(3):
                    out_f[side, c, pl.ds(i * 8 + k, 1), :] = row(c, idx)
        return carry

    lax.fori_loop(0, NF // 8, fill_face, 0)
    greeted(barrier, me_t)
    ask_b.start()
    ask_f.start()

    got_b[me_b, 0:3] = jnp.full((3, NS, NV), FAR, f32)
    got_b[me_b, 3] = jnp.zeros((NS, NV), f32)
    ret_b[me_b] = jnp.zeros((3, NS, NV), f32)

    @pl.when(me_t == 0)
    def _():
        got_f[0] = jnp.full((3, NF, NV), FAR, f32)
        ret_f[0] = jnp.zeros((3, NF, NV), f32)

    @pl.when(me_t == 3)
    def _():
        got_f[1] = jnp.full((3, NF, NV), FAR, f32)
        ret_f[1] = jnp.zeros((3, NF, NV), f32)

    def border(i, carry):
        for k in range(8):
            idx = pick[0, i * 8 + k]
            at = pl.ds(i * 8 + k, 1)
            for c in range(3):
                brd[c, at, :] = verts[c, pl.ds(idx, 1), :]
            brd[3, at, :] = stiff[pl.ds(idx, 1), :]
        return carry

    lax.fori_loop(0, NV // 8, border, 0)
    groups = Groups(xg, vg, sg, lx, lc, rx, rc, eb)

    def pushing(u, p, idx):
        for c in range(3):
            vg[u, c, p : p + 1, :] = verts[c, pl.ds(idx, 1), :]
        sg[u, p : p + 1, :] = stiff[pl.ds(idx, 1), :]

    def load_local(u, g):
        for p in range(8):
            a = loc[0, g * 8 + p]
            for c in range(3):
                xg[u, c, p : p + 1, :] = verts[c, pl.ds(a, 1), :]
            pushing(u, p, loc[1, g * 8 + p])

    def put_local(g, push, re):
        for c in range(3):
            push_l[c, rows8(g), :] = push[c]
            react[c, rows8(g), :] = re[c]

    groups.run(0, FIRST, load_local, put_local)

    ask_b.wait()
    ask_f.wait()
    table = jnp.concatenate([brd[c] for c in range(4)], 1)
    t1 = table.astype(bf16)
    r = table - t1.astype(f32)
    t2 = r.astype(bf16)
    t3 = (r - t2.astype(f32)).astype(bf16)
    parts = jnp.concatenate([t1, t2, t3], 0)
    lane = lax.broadcasted_iota(i32, (NV, NV), 1).astype(f32)
    for h in range(NBS // NV):
        want = jnp.concatenate([got_b[h * 16 + s, 3] for s in range(16)], 0)
        for s in range(16):
            meta[h * 16 + s] = got_b[h * 16 + s, 3]
        hot = jnp.where(want == lane, 1.0, 0.0).astype(bf16)
        v = jnp.dot(jnp.concatenate([hot] * 3, 1), parts, preferred_element_type=f32)
        for c in range(4):
            gv[c, h * NV : (h + 1) * NV, :] = v[:, c * NV : (c + 1) * NV]

    def load_brick(u, g):
        for c in range(3):
            xg[u, c] = got_b[g, c]
            vg[u, c] = gv[c, rows8(g), :]
        sg[u] = gv[3, rows8(g), :]

    def put_brick(g, push, re):
        for c in range(3):
            back_b[g, c] = push[c]
            react[c, rows8(g, NL), :] = re[c]

    groups.run(0, NB, load_brick, put_brick)
    give_b.start()

    half = NF // 8

    def load_face(u, g):
        side = g // half
        k = lax.rem(g, half)
        for c in range(3):
            xg[u, c] = got_f[side, c, rows8(k), :]
        for p in range(8):
            pushing(u, p, fpick[side, k * 8 + p])

    def put_face(g, push, re):
        side = g // half
        k = lax.rem(g, half)
        for c in range(3):
            back_f[side, c, rows8(k), :] = push[c]
            react[c, rows8(g, NL + NBS), :] = re[c]

    groups.run(0, 2 * half, load_face, put_face)
    give_f.start()
    groups.run(FIRST, NL // 8 - FIRST, load_local, put_local)
    give_b.wait()
    give_f.wait()


def pairs(rp, fp, loc, pick, fpick, rs, verts, stiff):
    sds = jax.ShapeDtypeStruct
    return pl.pallas_call(
        pair_kernel,
        name="pairs",
        out_shape=(
            sds((3, NL, NV), f32),
            sds((3, NL + NBS + 2 * NF, NV), f32),
            sds((NB, 3, NS, NV), f32),
            sds((2, 3, NF, NV), f32),
            sds((NB, NS, NV), f32),
        ),
        in_specs=[sm] * 5 + [vm] * 3,
        out_specs=(vm,) * 5,
        scratch_shapes=[
            pltpu.VMEM((NB, 4, NS, NV), f32),
            pltpu.VMEM((2, 3, NF, NV), f32),
            pltpu.VMEM((NB, 4, NS, NV), f32),
            pltpu.VMEM((2, 3, NF, NV), f32),
            pltpu.VMEM((NB, 3, NS, NV), f32),
            pltpu.VMEM((2, 3, NF, NV), f32),
            pltpu.VMEM((4, NV, NV), f32),
            pltpu.VMEM((4, NBS, NV), f32),
            pltpu.VMEM((U, 3, 8, NV), f32),
            pltpu.VMEM((U, 3, 8, NV), f32),
            pltpu.VMEM((U, 8, NV), f32),
            *[pltpu.VMEM((U, 64, NV), f32)] * 4,
            pltpu.VMEM((U, 4, 4, NV, NV), bf16),
            pltpu.SemaphoreType.DMA((4, NB)),
            pltpu.SemaphoreType.DMA((4, 2)),
        ],
        compiler_params=pltpu.CompilerParams(
            collective_id=0, has_side_effects=True, vmem_limit_bytes=48 << 20
        ),
    )(rp, fp, loc, pick, fpick, rs, verts, stiff)


def merge_kernel(rp, fp, loc, pick, fpick, push_l, react, ret_b, ret_f, meta, out, *acc):
    me_t = lax.axis_index("slab")
    p1, p2, r1, r2, brd = acc[0:3], acc[3:6], acc[6:9], acc[9:12], acc[12]
    zero = jnp.zeros((64, NV), f32)

    def clear(i, carry):
        for ref in acc[0:12]:
            ref[pl.ds(pl.multiple_of(i * 64, 64), 64), :] = zero
        return carry

    lax.fori_loop(0, NP // 64, clear, 0)

    lane = lax.broadcasted_iota(i32, (NV, NV), 1).astype(f32)
    hots = []
    for h in range(NBS // NV):
        want = jnp.concatenate([meta[h * 16 + s] for s in range(16)], 0)
        hots.append(jnp.where(want == lane, 1.0, 0.0).astype(bf16))
    hot = jnp.concatenate(hots, 0)
    got = jnp.concatenate([react[c, NL : NL + NBS, :] for c in range(3)], 1)
    g1 = got.astype(bf16)
    g2 = got - g1.astype(f32)
    g3 = g2 - g2.astype(bf16).astype(f32)
    parts = jnp.concatenate([g1, g2.astype(bf16), g3.astype(bf16)], 0)
    total = lax.dot_general(
        jnp.concatenate([hot] * 3, 0), parts, D0, preferred_element_type=f32
    )
    for c in range(3):
        brd[c] = total[:, c * NV : (c + 1) * NV]

    def add(refs, idx, values):
        at = pl.ds(idx, 1)
        for c in range(3):
            refs[c][at, :] += values[c]

    def one(i, carry):
        for h in range(2):
            j = i + h * NV
            at = pl.ds(j, 1)
            add(p1, loc[0, j], [push_l[c, at, :] for c in range(3)])
            add(r1, loc[1, j], [react[c, at, :] for c in range(3)])
            s = j // NS
            k = lax.rem(j, NS)
            idx = rp[k, s]
            some = [jnp.where(idx >= 0, ret_b[s, c, pl.ds(k, 1), :], 0.0) for c in range(3)]
            add(p2, jnp.maximum(idx, 0), some)
            if h == 0:
                add(r2, pick[0, i], [brd[c, pl.ds(i, 1), :] for c in range(3)])
            else:
                side = i // NF
                k = lax.rem(i, NF)
                at = pl.ds(NL + NBS + i, 1)
                add(r2, fpick[side, k], [react[c, at, :] for c in range(3)])
                idx = fp[side, k]
                idx = jnp.where(jnp.where(side == 0, me_t > 0, me_t < 3), idx, -1)
                some = [jnp.where(idx >= 0, ret_f[side, c, pl.ds(k, 1), :], 0.0) for c in range(3)]
                add(p2, jnp.maximum(idx, 0), some)
        return carry

    lax.fori_loop(0, NV, one, 0)

    def spread(i, carry):
        at = pl.ds(pl.multiple_of(i * 64, 64), 64)
        for c in range(3):
            r = r1[c][at, :] + r2[c][at, :]
            s = r + pltpu.roll(r, 1, 1) + pltpu.roll(r, 2, 1)
            out[c, at, :] = p1[c][at, :] + p2[c][at, :] + s * (1.0 / 3.0)
        return carry

    lax.fori_loop(0, NP // 64, spread, 0)


def merge(rp, fp, loc, pick, fpick, push_l, react, ret_b, ret_f, meta):
    return pl.pallas_call(
        merge_kernel,
        name="merge",
        out_shape=jax.ShapeDtypeStruct((3, NP, NV), f32),
        in_specs=[sm] * 5 + [vm] * 5,
        out_specs=vm,
        scratch_shapes=[pltpu.VMEM((NP, NV), f32)] * 12 + [pltpu.VMEM((3, NV, NV), f32)],
        compiler_params=pltpu.CompilerParams(vmem_limit_bytes=48 << 20),
    )(rp, fp, loc, pick, fpick, push_l, react, ret_b, ret_f, meta)


def body(verts, stiffness, local_pairs, border_pick, recv_src, recv_pair, face_pick, face_pair):
    rp = recv_pair[0].T
    lists = (rp, face_pair[0], local_pairs[0], border_pick, face_pick[0])
    made = pairs(*lists, recv_src[0].T, verts.transpose(1, 0, 2), stiffness)
    return merge(*lists, *made).transpose(1, 0, 2)


def solution(mesh):
    both = ("slab", "brick")
    placed = (
        P(both, None, None),
        P(both, None),
        P(both, None, None),
        P(both, None),
        P(both, None, None),
        P(both, None, None),
        P(both, None, None),
        P(both, None, None),
    )
    return jax.shard_map(
        body, mesh=mesh, in_specs=placed, out_specs=P(both, None, None), check_vma=False
    )
```

```python
import math

import jax
import jax.numpy as jnp
from jax import lax
from jax.experimental import pallas as pl
from jax.experimental.pallas import tpu as pltpu
from jax.sharding import PartitionSpec as P

f32 = jnp.float32
bf16 = jnp.bfloat16
i32 = jnp.int32
MESH = pl.DeviceIdType.MESH

NP = 1024
NV = 128
NB = 32
NS = 8
NF = 64
NBS = NB * NS
NL = 256
FIRST = 20
SQ = math.sqrt(math.log2(math.e))
FAR = 1.0e4
U = 4
CHUNKS = 4
LAG = 4
DN = (((1,), (1,)), ((), ()))
D0 = (((0,), (0,)), ((), ()))

vm = pl.BlockSpec(memory_space=pltpu.VMEM)
hbm = pl.BlockSpec(memory_space=pltpu.HBM)
LISTS = ((NS, NB), (2, NF), (2, NL), (1, NV), (2, NF))


def greet(me_t, me_b):
    sem = pltpu.get_barrier_semaphore()

    def one(o, c):
        pl.semaphore_signal(
            sem, inc=1, device_id=(me_t, lax.rem(me_b + o, NB)), device_id_type=MESH
        )
        return c

    lax.fori_loop(1, NB, one, 0)

    @pl.when(me_t > 0)
    def _():
        pl.semaphore_signal(sem, inc=1, device_id=(me_t - 1, me_b), device_id_type=MESH)

    @pl.when(me_t < 3)
    def _():
        pl.semaphore_signal(sem, inc=1, device_id=(me_t + 1, me_b), device_id_type=MESH)

    return sem


def greeted(sem, me_t):
    faces = (me_t > 0).astype(i32) + (me_t < 3).astype(i32)
    pl.semaphore_wait(sem, NB - 1 + faces)


class Brick:
    def __init__(self, src, dst, s_sem, r_sem, me_t, me_b):
        self.a = (src, dst, s_sem, r_sem, me_t, me_b)

    def copy(self, o, arrival=False):
        src, dst, s_sem, r_sem, me_t, me_b = self.a
        peer = lax.rem(me_b + o, NB)
        at = peer if arrival else me_b
        return pltpu.make_async_remote_copy(
            src_ref=src.at[peer],
            dst_ref=dst.at[at],
            send_sem=s_sem.at[peer],
            recv_sem=r_sem.at[at],
            device_id=(me_t, peer),
            device_id_type=MESH,
        )

    def start(self):
        def one(o, c):
            self.copy(o).start()
            return c

        lax.fori_loop(1, NB, one, 0)

    def wait(self):
        def one(o, c):
            self.copy(o, True).wait_recv()
            self.copy(o).wait_send()
            return c

        lax.fori_loop(1, NB, one, 0)


class Face:
    def __init__(self, src, dst, s_sem, r_sem, me_t, me_b):
        self.a = (src, dst, s_sem, r_sem, me_t, me_b)

    def copy(self, side, arrival=False):
        src, dst, s_sem, r_sem, me_t, me_b = self.a
        at = side if arrival else 1 - side
        return pltpu.make_async_remote_copy(
            src_ref=src.at[side],
            dst_ref=dst.at[at],
            send_sem=s_sem.at[side],
            recv_sem=r_sem.at[at],
            device_id=(me_t + (1 if side else -1), me_b),
            device_id_type=MESH,
        )

    def there(self, side):
        return (self.a[4] < 3) if side else (self.a[4] > 0)

    def start(self):
        for side in range(2):

            @pl.when(self.there(side))
            def _(side=side):
                self.copy(side).start()

    def wait(self):
        for side in range(2):

            @pl.when(self.there(side))
            def _(side=side):
                self.copy(side, True).wait_recv()
                self.copy(side).wait_send()


def split(x):
    high = x.astype(bf16).astype(f32)
    return high, x - high


def ahead(v, k):
    return pltpu.roll(v, NV - k, 1)


def prepare(xs, vs, stiff, lx, lc):
    one = jnp.ones((8, NV), f32)
    zero = jnp.zeros((8, NV), f32)
    cs = [(v + ahead(v, 1) + ahead(v, 2)) * (1.0 / 3.0) for v in vs]
    xp = [x * SQ for x in xs]
    cp = [c * SQ for c in cs]
    x1, x2 = zip(*[split(x) for x in xp])
    c1, c2 = zip(*[split(c) for c in cp])
    n = -0.5 * (xp[0] * xp[0] + xp[1] * xp[1] + xp[2] * xp[2])
    m = -0.5 * (cp[0] * cp[0] + cp[1] * cp[1] + cp[2] * cp[2]) + jnp.log2(stiff) - 7.0
    n1, r = split(n)
    n2, n3 = split(r)
    m1, r = split(m)
    m2, m3 = split(r)
    a = jnp.concatenate([*x1, *x1, *x2, n1, n2, n3, one, one, one, zero], 0).astype(bf16)
    b = jnp.concatenate([*c1, *c2, *c1, one, one, one, m1, m2, m3, zero], 0).astype(bf16)
    for ref, rows in ((lx, [*x1, *x2, one, zero]), (lc, [*c1, *c2, one, zero])):
        for k, r in enumerate(rows):
            ref[pl.ds(k, 8, stride=8), :] = r
    return cs, a.T, b


def energies(at, b, t):
    sub = lax.broadcasted_iota(i32, (NV, NV), 0) % 8
    zero = jnp.zeros_like(b)
    two = jnp.concatenate([jnp.where(sub == 2 * t + k, b, zero) for k in range(2)], 1)
    e = jnp.exp2(jnp.dot(at, two, preferred_element_type=f32))
    high = e.astype(bf16)
    return high, (e - high.astype(f32)).astype(bf16)


def sums(t, e, lx, lc, rx, rc):
    h0, l0, h1, l1 = e
    rows = slice(16 * t, 16 * t + 16)
    x = lx[rows, :].astype(bf16)
    c = lc[rows, :].astype(bf16)
    cat = jnp.concatenate
    e_ij = cat([cat([h0, h1], 1), cat([l0, l1], 1)], 0)
    e_ji = cat([cat([h0, l0], 1), cat([h1, l1], 1)], 0)
    r = jnp.dot(cat([x, x], 1), e_ij, preferred_element_type=f32)
    s = lax.dot_general(cat([c, c], 1), e_ji, DN, preferred_element_type=f32)
    for ref, v in ((rx, r), (rc, s)):
        ref[16 * t : 16 * t + 8, :] = v[0:8, 0:NV]
        ref[16 * t + 8 : 16 * t + 16, :] = v[8:16, NV : 2 * NV]


def forces(xs, cs, rx, rc):
    def get(ref, k):
        return ref[pl.ds(k, 8, stride=8), :]

    inv = 1.0 / SQ
    q = get(rx, 6)
    r = get(rc, 6)
    react = [cs[k] * q - (get(rx, k) + get(rx, 3 + k)) * inv for k in range(3)]
    push = [xs[k] * r - (get(rc, k) + get(rc, 3 + k)) * inv for k in range(3)]
    return push, react


class Groups:
    def __init__(self, xg, vg, sg, lx, lc, rx, rc, eb):
        self.r = (xg, vg, sg, lx, lc, rx, rc, eb)

    def run(self, first, count, load, put):
        xg, vg, sg, lx, lc, rx, rc, eb = self.r
        n = U * 4

        def second(i, g):
            u, t = divmod(i, 4)
            e = [eb[u, t, k] for k in range(4)]
            sums(t, e, lx.at[u], lc.at[u], rx.at[u], rc.at[u])
            if t == 3:
                xs = [xg[u, c] for c in range(3)]
                cs = [vg[u, c] for c in range(3)]
                put(g, *forces(xs, cs, rx.at[u], rc.at[u]))

        def step(s, carry):
            base = first + s * U
            for i in range(n):
                u, t = divmod(i, 4)
                if t == 0:
                    load(u, base + u)
                    xs = [xg[u, c] for c in range(3)]
                    cs, at, b = prepare(xs, [vg[u, c] for c in range(3)], sg[u], lx.at[u], lc.at[u])
                    for c in range(3):
                        vg[u, c] = cs[c]
                j = i - LAG
                ju = (j % n) // 4
                second(j % n, base + ju if j >= 0 else jnp.maximum(base + ju - U, first))
                high, low = energies(at, b, t)
                eb[u, t, 0] = high[:, :NV]
                eb[u, t, 1] = low[:, :NV]
                eb[u, t, 2] = high[:, NV:]
                eb[u, t, 3] = low[:, NV:]
            return carry

        lax.fori_loop(0, count // U, step, 0)
        for j in range(n - LAG, n):
            second(j, first + count - U + j // 4)


def rows8(g):
    return pl.ds(pl.multiple_of(g * 8, 8), 8)


def pair_kernel(
    *refs,
):
    ins, refs = refs[:8], refs[8:]
    outs, refs = refs[:5], refs[5:]
    ret_b, ret_f, *refs = refs
    here, refs = refs[:8], refs[8:]
    rp, fp, loc, pick, fpick, rs, verts, stiff = here
    made, refs = refs[:5], refs[5:]
    push_l, react_l, react_b, react_f, meta = made
    got_b, got_f, out_b, out_f, back_b, back_f, brd, gv, *work, sems, fsems, isems, osems = refs
    xg, vg, sg = work[:3]
    me_t = lax.axis_index("slab")
    me_b = lax.axis_index("brick")
    moves = [pltpu.make_async_copy(a, b, isems.at[k]) for k, (a, b) in enumerate(zip(ins, here))]
    for move in moves:
        move.start()
    barrier = greet(me_t, me_b)
    for move in moves:
        move.wait()
    ask_b = Brick(out_b, got_b, sems.at[0], sems.at[1], me_t, me_b)
    ask_f = Face(out_f, got_f, fsems.at[0], fsems.at[1], me_t, me_b)
    give_b = Brick(back_b, ret_b, sems.at[2], sems.at[3], me_t, me_b)
    give_f = Face(back_f, ret_f, fsems.at[2], fsems.at[3], me_t, me_b)

    def row(c, idx):
        return jnp.where(idx >= 0, verts[c, pl.ds(jnp.maximum(idx, 0), 1), :], FAR)

    def fill_brick(s, carry):
        for k in range(NS):
            idx = rp[k, s]
            for c in range(3):
                out_b[s, c, k : k + 1, :] = row(c, idx)
        return carry

    lax.fori_loop(0, NB, fill_brick, 0)
    for s in range(NB):
        out_b[s, 3] = jnp.broadcast_to(rs[:, s : s + 1].astype(f32), (NS, NV))

    def fill_face(i, carry):
        for side in range(2):
            for k in range(8):
                idx = fp[side, i * 8 + k]
                for c in range(3):
                    out_f[side, c, pl.ds(i * 8 + k, 1), :] = row(c, idx)
        return carry

    lax.fori_loop(0, NF // 8, fill_face, 0)
    greeted(barrier, me_t)
    ask_b.start()
    ask_f.start()

    got_b[me_b, 0:3] = jnp.full((3, NS, NV), FAR, f32)
    got_b[me_b, 3] = jnp.zeros((NS, NV), f32)

    @pl.when(me_t == 0)
    def _():
        got_f[0] = jnp.full((3, NF, NV), FAR, f32)

    @pl.when(me_t == 3)
    def _():
        got_f[1] = jnp.full((3, NF, NV), FAR, f32)

    def border(i, carry):
        for k in range(8):
            idx = pick[0, i * 8 + k]
            at = pl.ds(i * 8 + k, 1)
            for c in range(3):
                brd[c, at, :] = verts[c, pl.ds(idx, 1), :]
            brd[3, at, :] = stiff[pl.ds(idx, 1), :]
        return carry

    lax.fori_loop(0, NV // 8, border, 0)
    groups = Groups(*work)

    def pushing(u, p, idx):
        for c in range(3):
            vg[u, c, p : p + 1, :] = verts[c, pl.ds(idx, 1), :]
        sg[u, p : p + 1, :] = stiff[pl.ds(idx, 1), :]

    def load_local(u, g):
        for p in range(8):
            a = loc[0, g * 8 + p]
            for c in range(3):
                xg[u, c, p : p + 1, :] = verts[c, pl.ds(a, 1), :]
            pushing(u, p, loc[1, g * 8 + p])

    def put_local(g, push, re):
        for c in range(3):
            push_l[c, rows8(g), :] = push[c]
            react_l[c, rows8(g), :] = re[c]

    def out_copy(k, rows=None, slot=None):
        a, b = made[k], outs[k]
        if rows is not None:
            a, b = a.at[:, rows, :], b.at[:, rows, :]
        return pltpu.make_async_copy(a, b, osems.at[k if slot is None else slot])

    groups.run(0, FIRST, load_local, put_local)
    early = pl.ds(0, 8 * FIRST)
    late = pl.ds(8 * FIRST, NL - 8 * FIRST)
    copies = [out_copy(0, early), out_copy(1, early)]
    for copy in copies:
        copy.start()

    ask_b.wait()
    ask_f.wait()
    table = jnp.concatenate([brd[c] for c in range(4)], 1)
    t1 = table.astype(bf16)
    r = table - t1.astype(f32)
    t2 = r.astype(bf16)
    t3 = (r - t2.astype(f32)).astype(bf16)
    parts = jnp.concatenate([t1, t2, t3], 0)
    lane = lax.broadcasted_iota(i32, (NV, NV), 1).astype(f32)
    for h in range(NBS // NV):
        want = jnp.concatenate([got_b[h * 16 + s, 3] for s in range(16)], 0)
        for s in range(16):
            meta[h * 16 + s] = got_b[h * 16 + s, 3]
        hot = jnp.where(want == lane, 1.0, 0.0).astype(bf16)
        v = jnp.dot(jnp.concatenate([hot] * 3, 1), parts, preferred_element_type=f32)
        for c in range(4):
            gv[c, h * NV : (h + 1) * NV, :] = v[:, c * NV : (c + 1) * NV]

    def load_brick(u, g):
        for c in range(3):
            xg[u, c] = got_b[g, c]
            vg[u, c] = gv[c, rows8(g), :]
        sg[u] = gv[3, rows8(g), :]

    def put_brick(g, push, re):
        for c in range(3):
            back_b[g, c] = push[c]
            react_b[c, rows8(g), :] = re[c]

    groups.run(0, NB, load_brick, put_brick)
    give_b.start()
    copies += [out_copy(2), out_copy(4)]
    copies.append(pltpu.make_async_copy(back_b.at[me_b], ret_b.at[me_b], osems.at[7]))
    for copy in copies[2:]:
        copy.start()

    half = NF // 8

    def load_face(u, g):
        side = g // half
        k = lax.rem(g, half)
        for c in range(3):
            xg[u, c] = got_f[side, c, rows8(k), :]
        for p in range(8):
            pushing(u, p, fpick[side, k * 8 + p])

    def put_face(g, push, re):
        side = g // half
        k = lax.rem(g, half)
        for c in range(3):
            back_f[side, c, rows8(k), :] = push[c]
            react_f[c, rows8(g), :] = re[c]

    groups.run(0, 2 * half, load_face, put_face)
    give_f.start()
    copies.append(out_copy(3))
    copies[-1].start()
    ends = [pltpu.make_async_copy(back_f.at[k], ret_f.at[k], osems.at[8]) for k in range(2)]
    for side in range(2):

        @pl.when(jnp.logical_not(give_f.there(side)))
        def _(side=side):
            ends[side].start()

    groups.run(FIRST, NL // 8 - FIRST, load_local, put_local)
    copies += [out_copy(0, late, 5), out_copy(1, late, 6)]
    for copy in copies[-2:]:
        copy.start()
    give_b.wait()
    give_f.wait()
    for side in range(2):

        @pl.when(jnp.logical_not(give_f.there(side)))
        def _(side=side):
            ends[side].wait()

    for copy in copies:
        copy.wait()


MADE = ((3, NL, NV), (3, NL, NV), (3, NBS, NV), (3, 2 * NF, NV), (NB, NS, NV))
BACK = ((NB, 3, NS, NV), (2, 3, NF, NV))


def pairs(rp, fp, loc, pick, fpick, rs, verts, stiff):
    sds = jax.ShapeDtypeStruct
    return pl.pallas_call(
        pair_kernel,
        name="pairs",
        out_shape=tuple(sds(shape, f32) for shape in MADE + BACK),
        in_specs=[hbm] * 8,
        out_specs=(hbm,) * 7,
        scratch_shapes=[
            *[pltpu.SMEM(shape, i32) for shape in LISTS],
            pltpu.VMEM((NS, NB), i32),
            pltpu.VMEM((3, NP, NV), f32),
            pltpu.VMEM((NP, NV), f32),
            *[pltpu.VMEM(shape, f32) for shape in MADE],
            pltpu.VMEM((NB, 4, NS, NV), f32),
            pltpu.VMEM((2, 3, NF, NV), f32),
            pltpu.VMEM((NB, 4, NS, NV), f32),
            pltpu.VMEM((2, 3, NF, NV), f32),
            pltpu.VMEM((NB, 3, NS, NV), f32),
            pltpu.VMEM((2, 3, NF, NV), f32),
            pltpu.VMEM((4, NV, NV), f32),
            pltpu.VMEM((4, NBS, NV), f32),
            pltpu.VMEM((U, 3, 8, NV), f32),
            pltpu.VMEM((U, 3, 8, NV), f32),
            pltpu.VMEM((U, 8, NV), f32),
            *[pltpu.VMEM((U, 64, NV), f32)] * 4,
            pltpu.VMEM((U, 4, 4, NV, NV), bf16),
            pltpu.SemaphoreType.DMA((4, NB)),
            pltpu.SemaphoreType.DMA((4, 2)),
            pltpu.SemaphoreType.DMA((8,)),
            pltpu.SemaphoreType.DMA((9,)),
        ],
        compiler_params=pltpu.CompilerParams(collective_id=0, has_side_effects=True),
    )(rp, fp, loc, pick, fpick, rs, verts, stiff)


def flat(a):
    lane = lax.broadcasted_iota(i32, (NB, NBS), 1)
    wide = (lane // NS == lax.broadcasted_iota(i32, (NB, NBS), 0)).astype(f32).astype(bf16)
    high, low = split(a.astype(f32))
    row = jnp.dot(high.astype(bf16), wide, preferred_element_type=f32)
    row = row + jnp.dot(low.astype(bf16), wide, preferred_element_type=f32)
    own = lax.broadcasted_iota(i32, (NS, NBS), 0) == lax.broadcasted_iota(i32, (NS, NBS), 1) % NS
    return jnp.sum(jnp.where(own, row, 0.0), axis=0, keepdims=True)


def two(x):
    high, low = split(x)
    return high.astype(bf16), low.astype(bf16)


def side_by_side(a):
    return jnp.concatenate([a[0:1], a[1:2]], 1).astype(f32)


def merge_kernel(*refs):
    n_in = 5 + len(MADE) + len(BACK)
    ins, out, here, refs = refs[:n_in], refs[n_in], refs[n_in + 1 : 2 * n_in + 1], refs[2 * n_in + 1 :]
    rp, fp, loc, pick, fpick, push_l, react_l, react_b, react_f, meta, ret_b, ret_f = here
    made, isems, osems = refs
    moves = [pltpu.make_async_copy(a, b, isems.at[k]) for k, (a, b) in enumerate(zip(ins, here))]
    for move in moves:
        move.start()
    for move in moves:
        move.wait()
    cat = jnp.concatenate

    def lanes(ref):
        return cat([ref[c] for c in range(3)], 1)

    lane = lax.broadcasted_iota(i32, (NV, NV), 1).astype(f32)
    hots = []
    for h in range(NBS // NV):
        want = cat([meta[h * 16 + s] for s in range(16)], 0)
        hots.append(jnp.where(want == lane, 1.0, 0.0).astype(bf16))
    hot = cat(hots, 0)
    border = lax.dot_general(cat([hot] * 2, 0), cat(two(lanes(react_b)), 0), D0, preferred_element_type=f32)

    back_b = cat([cat([ret_b[s, c] for s in range(NB)], 0) for c in range(3)], 1)
    back_f = cat([cat([ret_f[k, c] for k in range(2)], 0) for c in range(3)], 1)
    push = cat(two(cat([lanes(push_l), back_b, back_f], 0)), 0)
    react = cat(two(cat([lanes(react_l), border, lanes(react_f)], 0)), 0)
    pushed = cat([loc[0:1].astype(f32), flat(rp[...]), side_by_side(fp[...])], 1)
    pushing = cat([loc[1:2].astype(f32), pick[...].astype(f32), side_by_side(fpick[...])], 1)

    size = NP // CHUNKS
    copies = []
    for n in range(CHUNKS):

        def scatter(idx, values):
            row = lax.broadcasted_iota(i32, (size, idx.shape[1]), 0).astype(f32) + float(n * size)
            one = jnp.where(row == idx, 1.0, 0.0).astype(bf16)
            return jnp.dot(cat([one, one], 1), values, preferred_element_type=f32)

        p = scatter(pushed, push)
        q = scatter(pushing, react)
        rows = pl.ds(n * size, size)
        for c in range(3):
            r = q[:, c * NV : (c + 1) * NV]
            s = r + pltpu.roll(r, 1, 1) + pltpu.roll(r, 2, 1)
            made[c, rows, :] = p[:, c * NV : (c + 1) * NV] + s * (1.0 / 3.0)
        copies.append(pltpu.make_async_copy(made.at[:, rows, :], out.at[:, rows, :], osems.at[n]))
        copies[-1].start()
    for copy in copies:
        copy.wait()


def merge(*args):
    return pl.pallas_call(
        merge_kernel,
        name="merge",
        out_shape=jax.ShapeDtypeStruct((3, NP, NV), f32),
        in_specs=[hbm] * len(args),
        out_specs=hbm,
        scratch_shapes=[
            *[pltpu.VMEM(shape, i32) for shape in LISTS],
            *[pltpu.VMEM(shape, f32) for shape in MADE + BACK],
            pltpu.VMEM((3, NP, NV), f32),
            pltpu.SemaphoreType.DMA((len(args),)),
            pltpu.SemaphoreType.DMA((CHUNKS,)),
        ],
    )(*args)


def body(verts, stiffness, local_pairs, border_pick, recv_src, recv_pair, face_pick, face_pair):
    rp = recv_pair[0].T
    lists = (rp, face_pair[0], local_pairs[0], border_pick, face_pick[0])
    made = pairs(*lists, recv_src[0].T, verts.transpose(1, 0, 2), stiffness)
    return merge(*lists, *made).transpose(1, 0, 2)


def solution(mesh):
    both = ("slab", "brick")
    placed = (
        P(both, None, None),
        P(both, None),
        P(both, None, None),
        P(both, None),
        P(both, None, None),
        P(both, None, None),
        P(both, None, None),
        P(both, None, None),
    )
    return jax.shard_map(
        body, mesh=mesh, in_specs=placed, out_specs=P(both, None, None), check_vma=False
    )
```

```python
import math

import jax
import jax.numpy as jnp
from jax import lax
from jax.experimental import pallas as pl
from jax.experimental.pallas import tpu as pltpu
from jax.sharding import PartitionSpec as P

f32 = jnp.float32
bf16 = jnp.bfloat16
i32 = jnp.int32
MESH = pl.DeviceIdType.MESH

NP = 1024
NV = 128
NB = 32
NS = 8
NF = 64
NBS = NB * NS
NL = 256
FIRST = 16
SQ = math.sqrt(math.log2(math.e))
FAR = 1.0e4
U = 4
CHUNKS = 4
LAG = 4
DN = (((1,), (1,)), ((), ()))
D0 = (((0,), (0,)), ((), ()))

vm = pl.BlockSpec(memory_space=pltpu.VMEM)
hbm = pl.BlockSpec(memory_space=pltpu.HBM)
LISTS = ((NS, NB), (2, NF), (2, NL), (1, NV), (2, NF))


def greet(me_t, me_b):
    sem = pltpu.get_barrier_semaphore()

    def one(o, c):
        pl.semaphore_signal(
            sem, inc=1, device_id=(me_t, lax.rem(me_b + o, NB)), device_id_type=MESH
        )
        return c

    lax.fori_loop(1, NB, one, 0)

    @pl.when(me_t > 0)
    def _():
        pl.semaphore_signal(sem, inc=1, device_id=(me_t - 1, me_b), device_id_type=MESH)

    @pl.when(me_t < 3)
    def _():
        pl.semaphore_signal(sem, inc=1, device_id=(me_t + 1, me_b), device_id_type=MESH)

    return sem


def greeted(sem, me_t):
    faces = (me_t > 0).astype(i32) + (me_t < 3).astype(i32)
    pl.semaphore_wait(sem, NB - 1 + faces)


class Brick:
    def __init__(self, src, dst, s_sem, r_sem, me_t, me_b):
        self.a = (src, dst, s_sem, r_sem, me_t, me_b)

    def copy(self, o, arrival=False):
        src, dst, s_sem, r_sem, me_t, me_b = self.a
        peer = lax.rem(me_b + o, NB)
        at = peer if arrival else me_b
        return pltpu.make_async_remote_copy(
            src_ref=src.at[peer],
            dst_ref=dst.at[at],
            send_sem=s_sem.at[peer],
            recv_sem=r_sem.at[at],
            device_id=(me_t, peer),
            device_id_type=MESH,
        )

    def start(self):
        def one(o, c):
            self.copy(o).start()
            return c

        lax.fori_loop(1, NB, one, 0)

    def wait(self):
        def one(o, c):
            self.copy(o, True).wait_recv()
            self.copy(o).wait_send()
            return c

        lax.fori_loop(1, NB, one, 0)


class Face:
    def __init__(self, src, dst, s_sem, r_sem, me_t, me_b):
        self.a = (src, dst, s_sem, r_sem, me_t, me_b)

    def copy(self, side, arrival=False):
        src, dst, s_sem, r_sem, me_t, me_b = self.a
        at = side if arrival else 1 - side
        return pltpu.make_async_remote_copy(
            src_ref=src.at[side],
            dst_ref=dst.at[at],
            send_sem=s_sem.at[side],
            recv_sem=r_sem.at[at],
            device_id=(me_t + (1 if side else -1), me_b),
            device_id_type=MESH,
        )

    def there(self, side):
        return (self.a[4] < 3) if side else (self.a[4] > 0)

    def start(self):
        for side in range(2):

            @pl.when(self.there(side))
            def _(side=side):
                self.copy(side).start()

    def wait(self):
        for side in range(2):

            @pl.when(self.there(side))
            def _(side=side):
                self.copy(side, True).wait_recv()
                self.copy(side).wait_send()


def split(x):
    high = x.astype(bf16).astype(f32)
    return high, x - high


def ahead(v, k):
    return pltpu.roll(v, NV - k, 1)


def prepare(xs, vs, stiff, lx, lc):
    one = jnp.ones((8, NV), f32)
    zero = jnp.zeros((8, NV), f32)
    cs = [(v + ahead(v, 1) + ahead(v, 2)) * (1.0 / 3.0) for v in vs]
    xp = [x * SQ for x in xs]
    cp = [c * SQ for c in cs]
    x1, x2 = zip(*[split(x) for x in xp])
    c1, c2 = zip(*[split(c) for c in cp])
    n = -0.5 * (xp[0] * xp[0] + xp[1] * xp[1] + xp[2] * xp[2])
    m = -0.5 * (cp[0] * cp[0] + cp[1] * cp[1] + cp[2] * cp[2]) + jnp.log2(stiff) - 7.0
    n1, r = split(n)
    n2, n3 = split(r)
    m1, r = split(m)
    m2, m3 = split(r)
    a = jnp.concatenate([*x1, *x1, *x2, n1, n2, n3, one, one, one, zero], 0).astype(bf16)
    b = jnp.concatenate([*c1, *c2, *c1, one, one, one, m1, m2, m3, zero], 0).astype(bf16)
    for ref, rows in ((lx, [*x1, *x2, one, zero]), (lc, [*c1, *c2, one, zero])):
        for k, r in enumerate(rows):
            ref[pl.ds(k, 8, stride=8), :] = r
    return cs, a.T, b


def energies(at, b, t):
    sub = lax.broadcasted_iota(i32, (NV, NV), 0) % 8
    zero = jnp.zeros_like(b)
    two = jnp.concatenate([jnp.where(sub == 2 * t + k, b, zero) for k in range(2)], 1)
    e = jnp.exp2(jnp.dot(at, two, preferred_element_type=f32))
    high = e.astype(bf16)
    return high, (e - high.astype(f32)).astype(bf16)


def sums(t, e, lx, lc, rx, rc):
    h0, l0, h1, l1 = e
    rows = slice(16 * t, 16 * t + 16)
    x = lx[rows, :].astype(bf16)
    c = lc[rows, :].astype(bf16)
    cat = jnp.concatenate
    e_ij = cat([cat([h0, h1], 1), cat([l0, l1], 1)], 0)
    e_ji = cat([cat([h0, l0], 1), cat([h1, l1], 1)], 0)
    r = jnp.dot(cat([x, x], 1), e_ij, preferred_element_type=f32)
    s = lax.dot_general(cat([c, c], 1), e_ji, DN, preferred_element_type=f32)
    for ref, v in ((rx, r), (rc, s)):
        ref[16 * t : 16 * t + 8, :] = v[0:8, 0:NV]
        ref[16 * t + 8 : 16 * t + 16, :] = v[8:16, NV : 2 * NV]


def forces(xs, cs, rx, rc):
    def get(ref, k):
        return ref[pl.ds(k, 8, stride=8), :]

    inv = 1.0 / SQ
    q = get(rx, 6)
    r = get(rc, 6)
    react = [cs[k] * q - (get(rx, k) + get(rx, 3 + k)) * inv for k in range(3)]
    push = [xs[k] * r - (get(rc, k) + get(rc, 3 + k)) * inv for k in range(3)]
    return push, react


class Groups:
    def __init__(self, xg, vg, sg, lx, lc, rx, rc, eb):
        self.r = (xg, vg, sg, lx, lc, rx, rc, eb)

    def run(self, first, count, load, put, after=None):
        xg, vg, sg, lx, lc, rx, rc, eb = self.r
        n = U * 4

        def second(i, g):
            u, t = divmod(i, 4)
            e = [eb[u, t, k] for k in range(4)]
            sums(t, e, lx.at[u], lc.at[u], rx.at[u], rc.at[u])
            if t == 3:
                xs = [xg[u, c] for c in range(3)]
                cs = [vg[u, c] for c in range(3)]
                put(g, *forces(xs, cs, rx.at[u], rc.at[u]))

        def step(s, carry):
            base = first + s * U
            for i in range(n):
                u, t = divmod(i, 4)
                if t == 0:
                    load(u, base + u)
                    xs = [xg[u, c] for c in range(3)]
                    cs, at, b = prepare(xs, [vg[u, c] for c in range(3)], sg[u], lx.at[u], lc.at[u])
                    for c in range(3):
                        vg[u, c] = cs[c]
                j = i - LAG
                ju = (j % n) // 4
                second(j % n, base + ju if j >= 0 else jnp.maximum(base + ju - U, first))
                high, low = energies(at, b, t)
                eb[u, t, 0] = high[:, :NV]
                eb[u, t, 1] = low[:, :NV]
                eb[u, t, 2] = high[:, NV:]
                eb[u, t, 3] = low[:, NV:]
            if after is not None:
                for u in range(U):
                    after(base + u - 1)
            return carry

        lax.fori_loop(0, count // U, step, 0)
        for j in range(n - LAG, n):
            second(j, first + count - U + j // 4)
        if after is not None:
            after(first + count - 1)


def rows8(g):
    return pl.ds(pl.multiple_of(g * 8, 8), 8)


def pair_kernel(
    *refs,
):
    ins, refs = refs[:8], refs[8:]
    outs, refs = refs[:5], refs[5:]
    ret_b, ret_f, *refs = refs
    here, refs = refs[:8], refs[8:]
    rp, fp, loc, pick, fpick, rs, verts, stiff = here
    made, refs = refs[:5], refs[5:]
    push_l, react_l, react_b, react_f, meta = made
    got_b, got_f, out_b, out_f, back_b, back_f, brd, gv, *work, sems, fsems, isems, osems = refs
    xg, vg, sg = work[:3]
    me_t = lax.axis_index("slab")
    me_b = lax.axis_index("brick")
    moves = [pltpu.make_async_copy(a, b, isems.at[k]) for k, (a, b) in enumerate(zip(ins, here))]
    for move in moves:
        move.start()
    barrier = greet(me_t, me_b)
    for move in moves:
        move.wait()
    ask_b = Brick(out_b, got_b, sems.at[0], sems.at[1], me_t, me_b)
    ask_f = Face(out_f, got_f, fsems.at[0], fsems.at[1], me_t, me_b)
    give_b = Brick(back_b, ret_b, sems.at[2], sems.at[3], me_t, me_b)
    give_f = Face(back_f, ret_f, fsems.at[2], fsems.at[3], me_t, me_b)

    def row(c, idx):
        return jnp.where(idx >= 0, verts[c, pl.ds(jnp.maximum(idx, 0), 1), :], FAR)

    for s in range(NB):
        out_b[s, 3] = jnp.broadcast_to(rs[:, s : s + 1].astype(f32), (NS, NV))
    got_b[me_b, 0:3] = jnp.full((3, NS, NV), FAR, f32)
    got_b[me_b, 3] = jnp.zeros((NS, NV), f32)

    @pl.when(me_t == 0)
    def _():
        got_f[0] = jnp.full((3, NF, NV), FAR, f32)

    @pl.when(me_t == 3)
    def _():
        got_f[1] = jnp.full((3, NF, NV), FAR, f32)

    groups = Groups(*work)
    half = NF // 8

    def pushing(u, p, idx):
        for c in range(3):
            vg[u, c, p : p + 1, :] = verts[c, pl.ds(idx, 1), :]
        sg[u, p : p + 1, :] = stiff[pl.ds(idx, 1), :]

    def load_local(u, g):
        for p in range(8):
            a = loc[0, g * 8 + p]
            for c in range(3):
                xg[u, c, p : p + 1, :] = verts[c, pl.ds(a, 1), :]
            pushing(u, p, loc[1, g * 8 + p])

    def load_first(u, g):
        load_local(u, g)
        for h in range(2):
            s = 2 * g + h
            for k in range(NS):
                for c in range(3):
                    out_b[s, c, k : k + 1, :] = row(c, rp[k, s])
        side = g // half
        for k in range(8):
            j = lax.rem(g, half) * 8 + k
            for c in range(3):
                out_f[side, c, pl.ds(j, 1), :] = row(c, fp[side, j])

    def load_second(u, g):
        load_local(u, g)
        for k in range(8):
            j = (g - FIRST) * 8 + k
            idx = pick[0, j]
            for c in range(3):
                brd[c, pl.ds(j, 1), :] = verts[c, pl.ds(idx, 1), :]
            brd[3, pl.ds(j, 1), :] = stiff[pl.ds(idx, 1), :]

    def put_local(g, push, re):
        for c in range(3):
            push_l[c, rows8(g), :] = push[c]
            react_l[c, rows8(g), :] = re[c]

    groups.run(0, FIRST, load_first, put_local)
    greeted(barrier, me_t)
    ask_f.start()
    ask_b.start()
    groups.run(FIRST, NL // 8 - FIRST, load_second, put_local)

    copies = []

    def give_out(k):
        copies.append(pltpu.make_async_copy(made[k], outs[k], osems.at[k]))
        copies[-1].start()

    give_out(0)
    give_out(1)

    def load_face(u, g):
        side = g // half
        k = lax.rem(g, half)
        for c in range(3):
            xg[u, c] = got_f[side, c, rows8(k), :]
        for p in range(8):
            pushing(u, p, fpick[side, k * 8 + p])

    def put_face(g, push, re):
        side = g // half
        k = lax.rem(g, half)
        for c in range(3):
            back_f[side, c, rows8(k), :] = push[c]
            react_f[c, rows8(g), :] = re[c]

    ask_f.wait()
    groups.run(0, 2 * half, load_face, put_face)
    give_f.start()
    give_out(3)
    ends = [pltpu.make_async_copy(back_f.at[k], ret_f.at[k], fsems.at[4, k]) for k in range(2)]
    for side in range(2):

        @pl.when(jnp.logical_not(give_f.there(side)))
        def _(side=side):
            ends[side].start()

    ask_b.wait()
    table = jnp.concatenate([brd[c] for c in range(4)], 1)
    t1 = table.astype(bf16)
    r = table - t1.astype(f32)
    t2 = r.astype(bf16)
    t3 = (r - t2.astype(f32)).astype(bf16)
    parts = jnp.concatenate([t1, t2, t3], 0)
    lane = lax.broadcasted_iota(i32, (NV, NV), 1).astype(f32)
    for h in range(NBS // NV):
        want = jnp.concatenate([got_b[h * 16 + s, 3] for s in range(16)], 0)
        for s in range(16):
            meta[h * 16 + s] = got_b[h * 16 + s, 3]
        hot = jnp.where(want == lane, 1.0, 0.0).astype(bf16)
        v = jnp.dot(jnp.concatenate([hot] * 3, 1), parts, preferred_element_type=f32)
        for c in range(4):
            gv[c, h * NV : (h + 1) * NV, :] = v[:, c * NV : (c + 1) * NV]

    give_out(4)

    def load_brick(u, o):
        s = lax.rem(me_b + o, NB)
        for c in range(3):
            xg[u, c] = got_b[s, c]
            vg[u, c] = gv[c, rows8(s), :]
        sg[u] = gv[3, rows8(s), :]

    def put_brick(o, push, re):
        s = lax.rem(me_b + o, NB)
        for c in range(3):
            back_b[s, c] = push[c]
            react_b[c, rows8(s), :] = re[c]

    def send_back(o):
        @pl.when(o >= 1)
        def _():
            give_b.copy(o).start()

    groups.run(0, NB, load_brick, put_brick, send_back)
    give_out(2)
    own = pltpu.make_async_copy(back_b.at[me_b], ret_b.at[me_b], osems.at[5])
    own.start()
    give_b.wait()
    give_f.wait()
    for side in range(2):

        @pl.when(jnp.logical_not(give_f.there(side)))
        def _(side=side):
            ends[side].wait()

    own.wait()
    for copy in copies:
        copy.wait()


MADE = ((3, NL, NV), (3, NL, NV), (3, NBS, NV), (3, 2 * NF, NV), (NB, NS, NV))
BACK = ((NB, 3, NS, NV), (2, 3, NF, NV))


def pairs(rp, fp, loc, pick, fpick, rs, verts, stiff):
    sds = jax.ShapeDtypeStruct
    return pl.pallas_call(
        pair_kernel,
        name="pairs",
        out_shape=tuple(sds(shape, f32) for shape in MADE + BACK),
        in_specs=[hbm] * 8,
        out_specs=(hbm,) * 7,
        scratch_shapes=[
            *[pltpu.SMEM(shape, i32) for shape in LISTS],
            pltpu.VMEM((NS, NB), i32),
            pltpu.VMEM((3, NP, NV), f32),
            pltpu.VMEM((NP, NV), f32),
            *[pltpu.VMEM(shape, f32) for shape in MADE],
            pltpu.VMEM((NB, 4, NS, NV), f32),
            pltpu.VMEM((2, 3, NF, NV), f32),
            pltpu.VMEM((NB, 4, NS, NV), f32),
            pltpu.VMEM((2, 3, NF, NV), f32),
            pltpu.VMEM((NB, 3, NS, NV), f32),
            pltpu.VMEM((2, 3, NF, NV), f32),
            pltpu.VMEM((4, NV, NV), f32),
            pltpu.VMEM((4, NBS, NV), f32),
            pltpu.VMEM((U, 3, 8, NV), f32),
            pltpu.VMEM((U, 3, 8, NV), f32),
            pltpu.VMEM((U, 8, NV), f32),
            *[pltpu.VMEM((U, 64, NV), f32)] * 4,
            pltpu.VMEM((U, 4, 4, NV, NV), bf16),
            pltpu.SemaphoreType.DMA((4, NB)),
            pltpu.SemaphoreType.DMA((5, 2)),
            pltpu.SemaphoreType.DMA((8,)),
            pltpu.SemaphoreType.DMA((6,)),
        ],
        compiler_params=pltpu.CompilerParams(collective_id=0, has_side_effects=True),
    )(rp, fp, loc, pick, fpick, rs, verts, stiff)


def flat(a):
    lane = lax.broadcasted_iota(i32, (NB, NBS), 1)
    wide = (lane // NS == lax.broadcasted_iota(i32, (NB, NBS), 0)).astype(f32).astype(bf16)
    high, low = split(a.astype(f32))
    row = jnp.dot(high.astype(bf16), wide, preferred_element_type=f32)
    row = row + jnp.dot(low.astype(bf16), wide, preferred_element_type=f32)
    own = lax.broadcasted_iota(i32, (NS, NBS), 0) == lax.broadcasted_iota(i32, (NS, NBS), 1) % NS
    return jnp.sum(jnp.where(own, row, 0.0), axis=0, keepdims=True)


def two(x):
    high, low = split(x)
    return high.astype(bf16), low.astype(bf16)


def side_by_side(a):
    return jnp.concatenate([a[0:1], a[1:2]], 1).astype(f32)


def merge_kernel(*refs):
    n_in = 5 + len(MADE) + len(BACK)
    ins, out, here, refs = refs[:n_in], refs[n_in], refs[n_in + 1 : 2 * n_in + 1], refs[2 * n_in + 1 :]
    rp, fp, loc, pick, fpick, push_l, react_l, react_b, react_f, meta, ret_b, ret_f = here
    made, isems, osems = refs
    moves = [pltpu.make_async_copy(a, b, isems.at[k]) for k, (a, b) in enumerate(zip(ins, here))]
    for move in moves:
        move.start()
    for move in moves:
        move.wait()
    cat = jnp.concatenate

    def lanes(ref):
        return cat([ref[c] for c in range(3)], 1)

    lane = lax.broadcasted_iota(i32, (NV, NV), 1).astype(f32)
    hots = []
    for h in range(NBS // NV):
        want = cat([meta[h * 16 + s] for s in range(16)], 0)
        hots.append(jnp.where(want == lane, 1.0, 0.0).astype(bf16))
    hot = cat(hots, 0)
    border = lax.dot_general(cat([hot] * 2, 0), cat(two(lanes(react_b)), 0), D0, preferred_element_type=f32)

    back_b = cat([cat([ret_b[s, c] for s in range(NB)], 0) for c in range(3)], 1)
    back_f = cat([cat([ret_f[k, c] for k in range(2)], 0) for c in range(3)], 1)
    push = cat(two(cat([lanes(push_l), back_b, back_f], 0)), 0)
    react = cat(two(cat([lanes(react_l), border, lanes(react_f)], 0)), 0)
    pushed = cat([loc[0:1].astype(f32), flat(rp[...]), side_by_side(fp[...])], 1)
    pushing = cat([loc[1:2].astype(f32), pick[...].astype(f32), side_by_side(fpick[...])], 1)

    size = NP // CHUNKS
    copies = []
    for n in range(CHUNKS):

        def scatter(idx, values):
            row = lax.broadcasted_iota(i32, (size, idx.shape[1]), 0).astype(f32) + float(n * size)
            one = jnp.where(row == idx, 1.0, 0.0).astype(bf16)
            return jnp.dot(cat([one, one], 1), values, preferred_element_type=f32)

        p = scatter(pushed, push)
        q = scatter(pushing, react)
        rows = pl.ds(n * size, size)
        for c in range(3):
            r = q[:, c * NV : (c + 1) * NV]
            s = r + pltpu.roll(r, 1, 1) + pltpu.roll(r, 2, 1)
            made[c, rows, :] = p[:, c * NV : (c + 1) * NV] + s * (1.0 / 3.0)
        copies.append(pltpu.make_async_copy(made.at[:, rows, :], out.at[:, rows, :], osems.at[n]))
        copies[-1].start()
    for copy in copies:
        copy.wait()


def merge(*args):
    return pl.pallas_call(
        merge_kernel,
        name="merge",
        out_shape=jax.ShapeDtypeStruct((3, NP, NV), f32),
        in_specs=[hbm] * len(args),
        out_specs=hbm,
        scratch_shapes=[
            *[pltpu.VMEM(shape, i32) for shape in LISTS],
            *[pltpu.VMEM(shape, f32) for shape in MADE + BACK],
            pltpu.VMEM((3, NP, NV), f32),
            pltpu.SemaphoreType.DMA((len(args),)),
            pltpu.SemaphoreType.DMA((CHUNKS,)),
        ],
    )(*args)


def body(verts, stiffness, local_pairs, border_pick, recv_src, recv_pair, face_pick, face_pair):
    rp = recv_pair[0].T
    lists = (rp, face_pair[0], local_pairs[0], border_pick, face_pick[0])
    made = pairs(*lists, recv_src[0].T, verts.transpose(1, 0, 2), stiffness)
    return merge(*lists, *made).transpose(1, 0, 2)


def solution(mesh):
    both = ("slab", "brick")
    placed = (
        P(both, None, None),
        P(both, None),
        P(both, None, None),
        P(both, None),
        P(both, None, None),
        P(both, None, None),
        P(both, None, None),
        P(both, None, None),
    )
    return jax.shard_map(
        body, mesh=mesh, in_specs=placed, out_specs=P(both, None, None), check_vma=False
    )
```

```python
import math

import jax
import jax.numpy as jnp
from jax import lax
from jax.experimental import pallas as pl
from jax.experimental.pallas import tpu as pltpu
from jax.sharding import PartitionSpec as P

f32 = jnp.float32
bf16 = jnp.bfloat16
i32 = jnp.int32
MESH = pl.DeviceIdType.MESH

NP = 1024
NV = 128
NB = 32
NS = 8
NF = 64
NBS = NB * NS
NL = 256
FIRST = 16
SECOND = 8
SQ = math.sqrt(math.log2(math.e))
FAR = 1.0e4
U = 16
CHUNKS = 4
LAG = 4
DN = (((1,), (1,)), ((), ()))
D0 = (((0,), (0,)), ((), ()))

vm = pl.BlockSpec(memory_space=pltpu.VMEM)
hbm = pl.BlockSpec(memory_space=pltpu.HBM)
LISTS = ((NS, NB), (2, NF), (2, NL), (1, NV), (2, NF))


def greet(me_t, me_b):
    sem = pltpu.get_barrier_semaphore()

    def one(o, c):
        pl.semaphore_signal(
            sem, inc=1, device_id=(me_t, lax.rem(me_b + o, NB)), device_id_type=MESH
        )
        return c

    lax.fori_loop(1, NB, one, 0)

    @pl.when(me_t > 0)
    def _():
        pl.semaphore_signal(sem, inc=1, device_id=(me_t - 1, me_b), device_id_type=MESH)

    @pl.when(me_t < 3)
    def _():
        pl.semaphore_signal(sem, inc=1, device_id=(me_t + 1, me_b), device_id_type=MESH)

    return sem


def greeted(sem, me_t):
    faces = (me_t > 0).astype(i32) + (me_t < 3).astype(i32)
    pl.semaphore_wait(sem, NB - 1 + faces)


class Brick:
    def __init__(self, src, dst, s_sem, r_sem, me_t, me_b):
        self.a = (src, dst, s_sem, r_sem, me_t, me_b)

    def copy(self, o, arrival=False):
        src, dst, s_sem, r_sem, me_t, me_b = self.a
        peer = lax.rem(me_b + o, NB)
        at = peer if arrival else me_b
        return pltpu.make_async_remote_copy(
            src_ref=src.at[peer],
            dst_ref=dst.at[at],
            send_sem=s_sem.at[peer],
            recv_sem=r_sem.at[at],
            device_id=(me_t, peer),
            device_id_type=MESH,
        )

    def start(self):
        def one(o, c):
            self.copy(o).start()
            return c

        lax.fori_loop(1, NB, one, 0)

    def wait(self):
        def one(o, c):
            self.copy(o, True).wait_recv()
            self.copy(o).wait_send()
            return c

        lax.fori_loop(1, NB, one, 0)


class Face:
    def __init__(self, src, dst, s_sem, r_sem, me_t, me_b):
        self.a = (src, dst, s_sem, r_sem, me_t, me_b)

    def copy(self, side, arrival=False):
        src, dst, s_sem, r_sem, me_t, me_b = self.a
        at = side if arrival else 1 - side
        return pltpu.make_async_remote_copy(
            src_ref=src.at[side],
            dst_ref=dst.at[at],
            send_sem=s_sem.at[side],
            recv_sem=r_sem.at[at],
            device_id=(me_t + (1 if side else -1), me_b),
            device_id_type=MESH,
        )

    def there(self, side):
        return (self.a[4] < 3) if side else (self.a[4] > 0)

    def start(self):
        for side in range(2):

            @pl.when(self.there(side))
            def _(side=side):
                self.copy(side).start()

    def wait(self):
        for side in range(2):

            @pl.when(self.there(side))
            def _(side=side):
                self.copy(side, True).wait_recv()
                self.copy(side).wait_send()


def split(x):
    high = x.astype(bf16).astype(f32)
    return high, x - high


def ahead(v, k):
    return pltpu.roll(v, NV - k, 1)


def prepare(xs, vs, stiff, lx, lc):
    one = jnp.ones((8, NV), f32)
    zero = jnp.zeros((8, NV), f32)
    cs = [(v + ahead(v, 1) + ahead(v, 2)) * (1.0 / 3.0) for v in vs]
    xp = [x * SQ for x in xs]
    cp = [c * SQ for c in cs]
    x1, x2 = zip(*[split(x) for x in xp])
    c1, c2 = zip(*[split(c) for c in cp])
    n = -0.5 * (xp[0] * xp[0] + xp[1] * xp[1] + xp[2] * xp[2])
    m = -0.5 * (cp[0] * cp[0] + cp[1] * cp[1] + cp[2] * cp[2]) + jnp.log2(stiff) - 7.0
    n1, r = split(n)
    n2, n3 = split(r)
    m1, r = split(m)
    m2, m3 = split(r)
    a = jnp.concatenate([*x1, *x1, *x2, n1, n2, n3, one, one, one, zero], 0).astype(bf16)
    b = jnp.concatenate([*c1, *c2, *c1, one, one, one, m1, m2, m3, zero], 0).astype(bf16)
    for ref, rows in ((lx, [*x1, *x2, one, zero]), (lc, [*c1, *c2, one, zero])):
        for k, r in enumerate(rows):
            ref[pl.ds(k, 8, stride=8), :] = r
    return cs, a.T, b


def energies(at, b, t):
    sub = lax.broadcasted_iota(i32, (NV, NV), 0) % 8
    zero = jnp.zeros_like(b)
    two = jnp.concatenate([jnp.where(sub == 2 * t + k, b, zero) for k in range(2)], 1)
    e = jnp.exp2(jnp.dot(at, two, preferred_element_type=f32))
    high = e.astype(bf16)
    return high, (e - high.astype(f32)).astype(bf16)


def sums(t, e, lx, lc, rx, rc):
    h0, l0, h1, l1 = e
    rows = slice(16 * t, 16 * t + 16)
    x = lx[rows, :].astype(bf16)
    c = lc[rows, :].astype(bf16)
    cat = jnp.concatenate
    e_ij = cat([cat([h0, h1], 1), cat([l0, l1], 1)], 0)
    e_ji = cat([cat([h0, l0], 1), cat([h1, l1], 1)], 0)
    r = jnp.dot(cat([x, x], 1), e_ij, preferred_element_type=f32)
    s = lax.dot_general(cat([c, c], 1), e_ji, DN, preferred_element_type=f32)
    for ref, v in ((rx, r), (rc, s)):
        ref[16 * t : 16 * t + 8, :] = v[0:8, 0:NV]
        ref[16 * t + 8 : 16 * t + 16, :] = v[8:16, NV : 2 * NV]


def forces(xs, cs, rx, rc):
    def get(ref, k):
        return ref[pl.ds(k, 8, stride=8), :]

    inv = 1.0 / SQ
    q = get(rx, 6)
    r = get(rc, 6)
    react = [cs[k] * q - (get(rx, k) + get(rx, 3 + k)) * inv for k in range(3)]
    push = [xs[k] * r - (get(rc, k) + get(rc, 3 + k)) * inv for k in range(3)]
    return push, react


class Groups:
    def __init__(self, xg, vg, sg, lx, lc, rx, rc, eb):
        self.r = (xg, vg, sg, lx, lc, rx, rc, eb)

    def second(self, i, g, put):
        xg, vg, sg, lx, lc, rx, rc, eb = self.r
        u, t = divmod(i, 4)
        e = [eb[u, t, k] for k in range(4)]
        sums(t, e, lx.at[u], lc.at[u], rx.at[u], rc.at[u])
        if t == 3:
            xs = [xg[u, c] for c in range(3)]
            cs = [vg[u, c] for c in range(3)]
            put(g, *forces(xs, cs, rx.at[u], rc.at[u]))

    def phase(self, base, count, load, put, before=None):
        xg, vg, sg, lx, lc, rx, rc, eb = self.r
        for i in range(count * 4):
            u, t = divmod(i, 4)
            if t == 0:
                load(u, base + u)
                xs = [xg[u, c] for c in range(3)]
                cs, at, b = prepare(xs, [vg[u, c] for c in range(3)], sg[u], lx.at[u], lc.at[u])
                for c in range(3):
                    vg[u, c] = cs[c]
            j = i - LAG
            if j >= 0:
                self.second(j, base + j // 4, put)
            elif before is not None:
                n, last, put_last = before
                self.second(n * 4 + j, last, put_last)
            high, low = energies(at, b, t)
            eb[u, t, 0] = high[:, :NV]
            eb[u, t, 1] = low[:, :NV]
            eb[u, t, 2] = high[:, NV:]
            eb[u, t, 3] = low[:, NV:]
        return count, base + count - 1, put

    def flush(self, before):
        n, last, put = before
        for j in range(n * 4 - LAG, n * 4):
            self.second(j, last, put)

    def loop(self, total, count, load, put, after):
        def step(s, carry):
            base = s * count
            self.phase(base, count, load, put, (count, jnp.maximum(base - 1, 0), put))
            for u in range(count):
                after(base + u - 1)
            return carry

        lax.fori_loop(0, total // count, step, 0)
        self.flush((count, total - 1, put))
        after(total - 1)


def rows8(g):
    return pl.ds(pl.multiple_of(g * 8, 8), 8)


def pair_kernel(
    *refs,
):
    ins, refs = refs[:8], refs[8:]
    outs, refs = refs[:5], refs[5:]
    ret_b, ret_f, *refs = refs
    here, refs = refs[:8], refs[8:]
    rp, fp, loc, pick, fpick, rs, verts, stiff = here
    made, refs = refs[:5], refs[5:]
    push_l, react_l, react_b, react_f, meta = made
    got_b, got_f, out_b, out_f, back_b, back_f, brd, gv, *work, sems, fsems, isems, osems = refs
    xg, vg, sg = work[:3]
    me_t = lax.axis_index("slab")
    me_b = lax.axis_index("brick")
    moves = [pltpu.make_async_copy(a, b, isems.at[k]) for k, (a, b) in enumerate(zip(ins, here))]
    for move in moves:
        move.start()
    barrier = greet(me_t, me_b)
    for move in moves:
        move.wait()
    ask_b = Brick(out_b, got_b, sems.at[0], sems.at[1], me_t, me_b)
    ask_f = Face(out_f, got_f, fsems.at[0], fsems.at[1], me_t, me_b)
    give_b = Brick(back_b, ret_b, sems.at[2], sems.at[3], me_t, me_b)
    give_f = Face(back_f, ret_f, fsems.at[2], fsems.at[3], me_t, me_b)

    def row(c, idx):
        return jnp.where(idx >= 0, verts[c, pl.ds(jnp.maximum(idx, 0), 1), :], FAR)

    for s in range(NB):
        out_b[s, 3] = jnp.broadcast_to(rs[:, s : s + 1].astype(f32), (NS, NV))
    got_b[me_b, 0:3] = jnp.full((3, NS, NV), FAR, f32)
    got_b[me_b, 3] = jnp.zeros((NS, NV), f32)

    @pl.when(me_t == 0)
    def _():
        got_f[0] = jnp.full((3, NF, NV), FAR, f32)

    @pl.when(me_t == 3)
    def _():
        got_f[1] = jnp.full((3, NF, NV), FAR, f32)

    groups = Groups(*work)
    half = NF // 8

    def pushing(u, p, idx):
        for c in range(3):
            vg[u, c, p : p + 1, :] = verts[c, pl.ds(idx, 1), :]
        sg[u, p : p + 1, :] = stiff[pl.ds(idx, 1), :]

    def load_local(u, g):
        for p in range(8):
            a = loc[0, g * 8 + p]
            for c in range(3):
                xg[u, c, p : p + 1, :] = verts[c, pl.ds(a, 1), :]
            pushing(u, p, loc[1, g * 8 + p])

    def load_first(u, g):
        load_local(u, g)
        for h in range(2):
            s = 2 * g + h
            for k in range(NS):
                for c in range(3):
                    out_b[s, c, k : k + 1, :] = row(c, rp[k, s])
        side = g // half
        for k in range(8):
            j = lax.rem(g, half) * 8 + k
            for c in range(3):
                out_f[side, c, pl.ds(j, 1), :] = row(c, fp[side, j])

    def load_second(u, g):
        load_local(u, g)
        for k in range(16):
            j = (g - FIRST) * 16 + k
            idx = pick[0, j]
            for c in range(3):
                brd[c, pl.ds(j, 1), :] = verts[c, pl.ds(idx, 1), :]
            brd[3, pl.ds(j, 1), :] = stiff[pl.ds(idx, 1), :]

    def put_local(g, push, re):
        for c in range(3):
            push_l[c, rows8(g), :] = push[c]
            react_l[c, rows8(g), :] = re[c]

    tail = groups.phase(0, FIRST, load_first, put_local)
    greeted(barrier, me_t)
    ask_f.start()
    ask_b.start()
    tail = groups.phase(FIRST, SECOND, load_second, put_local, tail)
    copies = []

    def give_out(k):
        copies.append(pltpu.make_async_copy(made[k], outs[k], osems.at[k]))
        copies[-1].start()

    def load_face(u, g):
        side = g // half
        k = lax.rem(g, half)
        for c in range(3):
            xg[u, c] = got_f[side, c, rows8(k), :]
        for p in range(8):
            pushing(u, p, fpick[side, k * 8 + p])

    def put_face(g, push, re):
        side = g // half
        k = lax.rem(g, half)
        for c in range(3):
            back_f[side, c, rows8(k), :] = push[c]
            react_f[c, rows8(g), :] = re[c]

    ask_f.wait()
    groups.flush(groups.phase(0, 2 * half, load_face, put_face, tail))
    give_f.start()
    give_out(3)
    ends = [pltpu.make_async_copy(back_f.at[k], ret_f.at[k], fsems.at[4, k]) for k in range(2)]
    for side in range(2):

        @pl.when(jnp.logical_not(give_f.there(side)))
        def _(side=side):
            ends[side].start()

    ask_b.wait()
    table = jnp.concatenate([brd[c] for c in range(4)], 1)
    t1 = table.astype(bf16)
    r = table - t1.astype(f32)
    t2 = r.astype(bf16)
    t3 = (r - t2.astype(f32)).astype(bf16)
    parts = jnp.concatenate([t1, t2, t3], 0)
    lane = lax.broadcasted_iota(i32, (NV, NV), 1).astype(f32)
    for h in range(NBS // NV):
        want = jnp.concatenate([got_b[h * 16 + s, 3] for s in range(16)], 0)
        for s in range(16):
            meta[h * 16 + s] = got_b[h * 16 + s, 3]
        hot = jnp.where(want == lane, 1.0, 0.0).astype(bf16)
        v = jnp.dot(jnp.concatenate([hot] * 3, 1), parts, preferred_element_type=f32)
        for c in range(4):
            gv[c, h * NV : (h + 1) * NV, :] = v[:, c * NV : (c + 1) * NV]

    give_out(4)

    def load_brick(u, o):
        s = lax.rem(me_b + o, NB)
        for c in range(3):
            xg[u, c] = got_b[s, c]
            vg[u, c] = gv[c, rows8(s), :]
        sg[u] = gv[3, rows8(s), :]

    def put_brick(o, push, re):
        s = lax.rem(me_b + o, NB)
        for c in range(3):
            back_b[s, c] = push[c]
            react_b[c, rows8(s), :] = re[c]

    def send_back(o):
        @pl.when(o >= 1)
        def _():
            give_b.copy(o).start()

    groups.loop(NB, U, load_brick, put_brick, send_back)
    give_out(2)
    own = pltpu.make_async_copy(back_b.at[me_b], ret_b.at[me_b], osems.at[5])
    own.start()
    late = FIRST + SECOND
    groups.flush(groups.phase(late, NL // 8 - late, load_local, put_local))
    give_out(0)
    give_out(1)
    give_b.wait()
    give_f.wait()
    for side in range(2):

        @pl.when(jnp.logical_not(give_f.there(side)))
        def _(side=side):
            ends[side].wait()

    own.wait()
    for copy in copies:
        copy.wait()


MADE = ((3, NL, NV), (3, NL, NV), (3, NBS, NV), (3, 2 * NF, NV), (NB, NS, NV))
BACK = ((NB, 3, NS, NV), (2, 3, NF, NV))


def pairs(rp, fp, loc, pick, fpick, rs, verts, stiff):
    sds = jax.ShapeDtypeStruct
    return pl.pallas_call(
        pair_kernel,
        name="pairs",
        out_shape=tuple(sds(shape, f32) for shape in MADE + BACK),
        in_specs=[hbm] * 8,
        out_specs=(hbm,) * 7,
        scratch_shapes=[
            *[pltpu.SMEM(shape, i32) for shape in LISTS],
            pltpu.VMEM((NS, NB), i32),
            pltpu.VMEM((3, NP, NV), f32),
            pltpu.VMEM((NP, NV), f32),
            *[pltpu.VMEM(shape, f32) for shape in MADE],
            pltpu.VMEM((NB, 4, NS, NV), f32),
            pltpu.VMEM((2, 3, NF, NV), f32),
            pltpu.VMEM((NB, 4, NS, NV), f32),
            pltpu.VMEM((2, 3, NF, NV), f32),
            pltpu.VMEM((NB, 3, NS, NV), f32),
            pltpu.VMEM((2, 3, NF, NV), f32),
            pltpu.VMEM((4, NV, NV), f32),
            pltpu.VMEM((4, NBS, NV), f32),
            pltpu.VMEM((U, 3, 8, NV), f32),
            pltpu.VMEM((U, 3, 8, NV), f32),
            pltpu.VMEM((U, 8, NV), f32),
            *[pltpu.VMEM((U, 64, NV), f32)] * 4,
            pltpu.VMEM((U, 4, 4, NV, NV), bf16),
            pltpu.SemaphoreType.DMA((4, NB)),
            pltpu.SemaphoreType.DMA((5, 2)),
            pltpu.SemaphoreType.DMA((8,)),
            pltpu.SemaphoreType.DMA((6,)),
        ],
        compiler_params=pltpu.CompilerParams(collective_id=0, has_side_effects=True),
    )(rp, fp, loc, pick, fpick, rs, verts, stiff)


def flat(a):
    lane = lax.broadcasted_iota(i32, (NB, NBS), 1)
    wide = (lane // NS == lax.broadcasted_iota(i32, (NB, NBS), 0)).astype(f32).astype(bf16)
    high, low = split(a.astype(f32))
    row = jnp.dot(high.astype(bf16), wide, preferred_element_type=f32)
    row = row + jnp.dot(low.astype(bf16), wide, preferred_element_type=f32)
    own = lax.broadcasted_iota(i32, (NS, NBS), 0) == lax.broadcasted_iota(i32, (NS, NBS), 1) % NS
    return jnp.sum(jnp.where(own, row, 0.0), axis=0, keepdims=True)


def two(x):
    high, low = split(x)
    return high.astype(bf16), low.astype(bf16)


def side_by_side(a):
    return jnp.concatenate([a[0:1], a[1:2]], 1).astype(f32)


def merge_kernel(*refs):
    n_in = 5 + len(MADE) + len(BACK)
    ins, out, here, refs = refs[:n_in], refs[n_in], refs[n_in + 1 : 2 * n_in + 1], refs[2 * n_in + 1 :]
    rp, fp, loc, pick, fpick, push_l, react_l, react_b, react_f, meta, ret_b, ret_f = here
    made, isems, osems = refs
    moves = [pltpu.make_async_copy(a, b, isems.at[k]) for k, (a, b) in enumerate(zip(ins, here))]
    for move in moves:
        move.start()
    for move in moves:
        move.wait()
    cat = jnp.concatenate

    def lanes(ref):
        return cat([ref[c] for c in range(3)], 1)

    lane = lax.broadcasted_iota(i32, (NV, NV), 1).astype(f32)
    hots = []
    for h in range(NBS // NV):
        want = cat([meta[h * 16 + s] for s in range(16)], 0)
        hots.append(jnp.where(want == lane, 1.0, 0.0).astype(bf16))
    hot = cat(hots, 0)
    border = lax.dot_general(cat([hot] * 2, 0), cat(two(lanes(react_b)), 0), D0, preferred_element_type=f32)

    back_b = cat([cat([ret_b[s, c] for s in range(NB)], 0) for c in range(3)], 1)
    back_f = cat([cat([ret_f[k, c] for k in range(2)], 0) for c in range(3)], 1)
    push = cat(two(cat([lanes(push_l), back_b, back_f], 0)), 0)
    react = cat(two(cat([lanes(react_l), border, lanes(react_f)], 0)), 0)
    pushed = cat([loc[0:1].astype(f32), flat(rp[...]), side_by_side(fp[...])], 1)
    pushing = cat([loc[1:2].astype(f32), pick[...].astype(f32), side_by_side(fpick[...])], 1)

    size = NP // CHUNKS
    copies = []
    for n in range(CHUNKS):

        def scatter(idx, values):
            row = lax.broadcasted_iota(i32, (size, idx.shape[1]), 0).astype(f32) + float(n * size)
            one = jnp.where(row == idx, 1.0, 0.0).astype(bf16)
            return jnp.dot(cat([one, one], 1), values, preferred_element_type=f32)

        p = scatter(pushed, push)
        q = scatter(pushing, react)
        rows = pl.ds(n * size, size)
        for c in range(3):
            r = q[:, c * NV : (c + 1) * NV]
            s = r + pltpu.roll(r, 1, 1) + pltpu.roll(r, 2, 1)
            made[c, rows, :] = p[:, c * NV : (c + 1) * NV] + s * (1.0 / 3.0)
        copies.append(pltpu.make_async_copy(made.at[:, rows, :], out.at[:, rows, :], osems.at[n]))
        copies[-1].start()
    for copy in copies:
        copy.wait()


def merge(*args):
    return pl.pallas_call(
        merge_kernel,
        name="merge",
        out_shape=jax.ShapeDtypeStruct((3, NP, NV), f32),
        in_specs=[hbm] * len(args),
        out_specs=hbm,
        scratch_shapes=[
            *[pltpu.VMEM(shape, i32) for shape in LISTS],
            *[pltpu.VMEM(shape, f32) for shape in MADE + BACK],
            pltpu.VMEM((3, NP, NV), f32),
            pltpu.SemaphoreType.DMA((len(args),)),
            pltpu.SemaphoreType.DMA((CHUNKS,)),
        ],
    )(*args)


def body(verts, stiffness, local_pairs, border_pick, recv_src, recv_pair, face_pick, face_pair):
    rp = recv_pair[0].T
    lists = (rp, face_pair[0], local_pairs[0], border_pick, face_pick[0])
    made = pairs(*lists, recv_src[0].T, verts.transpose(1, 0, 2), stiffness)
    return merge(*lists, *made).transpose(1, 0, 2)


def solution(mesh):
    both = ("slab", "brick")
    placed = (
        P(both, None, None),
        P(both, None),
        P(both, None, None),
        P(both, None),
        P(both, None, None),
        P(both, None, None),
        P(both, None, None),
        P(both, None, None),
    )
    return jax.shard_map(
        body, mesh=mesh, in_specs=placed, out_specs=P(both, None, None), check_vma=False
    )
```

```python
import math

import jax
import jax.numpy as jnp
from jax import lax
from jax.experimental import pallas as pl
from jax.experimental.pallas import tpu as pltpu
from jax.sharding import PartitionSpec as P

f32 = jnp.float32
bf16 = jnp.bfloat16
i32 = jnp.int32
MESH = pl.DeviceIdType.MESH

NP = 1024
NV = 128
NB = 32
NS = 8
NF = 64
NBS = NB * NS
NL = 256
FIRST = 16
SECOND = 8
SQ = math.sqrt(math.log2(math.e))
FAR = 1.0e4
U = 16
CHUNKS = 4
LAG = 4
DN = (((1,), (1,)), ((), ()))
D0 = (((0,), (0,)), ((), ()))

vm = pl.BlockSpec(memory_space=pltpu.VMEM)
hbm = pl.BlockSpec(memory_space=pltpu.HBM)
LISTS = ((NS, NB), (2, NF), (2, NL), (1, NV), (2, NF))


def greet(me_t, me_b):
    sem = pltpu.get_barrier_semaphore()

    def one(o, c):
        pl.semaphore_signal(
            sem, inc=1, device_id=(me_t, lax.rem(me_b + o, NB)), device_id_type=MESH
        )
        return c

    lax.fori_loop(1, NB, one, 0)

    @pl.when(me_t > 0)
    def _():
        pl.semaphore_signal(sem, inc=1, device_id=(me_t - 1, me_b), device_id_type=MESH)

    @pl.when(me_t < 3)
    def _():
        pl.semaphore_signal(sem, inc=1, device_id=(me_t + 1, me_b), device_id_type=MESH)

    return sem


def greeted(sem, me_t):
    faces = (me_t > 0).astype(i32) + (me_t < 3).astype(i32)
    pl.semaphore_wait(sem, NB - 1 + faces)


class Brick:
    def __init__(self, src, dst, s_sem, r_sem, me_t, me_b):
        self.a = (src, dst, s_sem, r_sem, me_t, me_b)

    def copy(self, o, arrival=False):
        src, dst, s_sem, r_sem, me_t, me_b = self.a
        peer = lax.rem(me_b + o, NB)
        at = peer if arrival else me_b
        return pltpu.make_async_remote_copy(
            src_ref=src.at[peer],
            dst_ref=dst.at[at],
            send_sem=s_sem.at[peer],
            recv_sem=r_sem.at[at],
            device_id=(me_t, peer),
            device_id_type=MESH,
        )

    def start(self):
        def one(o, c):
            self.copy(o).start()
            return c

        lax.fori_loop(1, NB, one, 0)

    def wait(self):
        def one(o, c):
            self.copy(o, True).wait_recv()
            self.copy(o).wait_send()
            return c

        lax.fori_loop(1, NB, one, 0)


class Face:
    def __init__(self, src, dst, s_sem, r_sem, me_t, me_b):
        self.a = (src, dst, s_sem, r_sem, me_t, me_b)

    def copy(self, side, arrival=False):
        src, dst, s_sem, r_sem, me_t, me_b = self.a
        at = side if arrival else 1 - side
        return pltpu.make_async_remote_copy(
            src_ref=src.at[side],
            dst_ref=dst.at[at],
            send_sem=s_sem.at[side],
            recv_sem=r_sem.at[at],
            device_id=(me_t + (1 if side else -1), me_b),
            device_id_type=MESH,
        )

    def there(self, side):
        return (self.a[4] < 3) if side else (self.a[4] > 0)

    def start(self):
        for side in range(2):

            @pl.when(self.there(side))
            def _(side=side):
                self.copy(side).start()

    def wait(self):
        for side in range(2):

            @pl.when(self.there(side))
            def _(side=side):
                self.copy(side, True).wait_recv()
                self.copy(side).wait_send()


def split(x):
    high = x.astype(bf16).astype(f32)
    return high, x - high


def ahead(v, k):
    return pltpu.roll(v, NV - k, 1)


def prepare(xs, vs, stiff, lx, lc, ab):
    one = jnp.ones((8, NV), f32)
    zero = jnp.zeros((8, NV), f32)
    cs = [(v + ahead(v, 1) + ahead(v, 2)) * (1.0 / 3.0) for v in vs]
    xp = [x * SQ for x in xs]
    cp = [c * SQ for c in cs]
    x1, x2 = zip(*[split(x) for x in xp])
    c1, c2 = zip(*[split(c) for c in cp])
    n = -0.5 * (xp[0] * xp[0] + xp[1] * xp[1] + xp[2] * xp[2])
    m = -0.5 * (cp[0] * cp[0] + cp[1] * cp[1] + cp[2] * cp[2]) + jnp.log2(stiff) - 7.0
    n1, r = split(n)
    n2, n3 = split(r)
    m1, r = split(m)
    m2, m3 = split(r)
    for k, r in enumerate([*x1, *x1, *x2, n1, n2, n3, one, one, one, zero]):
        ab[0, 8 * k : 8 * k + 8, :] = r
    for k, r in enumerate([*c1, *c2, *c1, one, one, one, m1, m2, m3, zero]):
        ab[1, 8 * k : 8 * k + 8, :] = r
    for ref, rows in ((lx, [*x1, *x2, one, zero]), (lc, [*c1, *c2, one, zero])):
        for k, r in enumerate(rows):
            ref[pl.ds(k, 8, stride=8), :] = r
    return cs


def energies(ab, t):
    def get(side, p):
        return ab[side, pl.ds(p, 16, stride=8), :].astype(bf16)

    cat = jnp.concatenate
    a = cat([get(0, 2 * t), get(0, 2 * t + 1)], 0).T
    b0 = get(1, 2 * t)
    b1 = get(1, 2 * t + 1)
    zero = jnp.zeros_like(b0)
    b = cat([cat([b0, zero], 1), cat([zero, b1], 1)], 0)
    e = jnp.exp2(jnp.dot(a, b, preferred_element_type=f32))
    high = e.astype(bf16)
    return high, (e - high.astype(f32)).astype(bf16)


def sums(t, e, lx, lc, rx, rc):
    h0, l0, h1, l1 = e
    rows = slice(16 * t, 16 * t + 16)
    x = lx[rows, :].astype(bf16)
    c = lc[rows, :].astype(bf16)
    cat = jnp.concatenate
    e_ij = cat([cat([h0, h1], 1), cat([l0, l1], 1)], 0)
    e_ji = cat([cat([h0, l0], 1), cat([h1, l1], 1)], 0)
    r = jnp.dot(cat([x, x], 1), e_ij, preferred_element_type=f32)
    s = lax.dot_general(cat([c, c], 1), e_ji, DN, preferred_element_type=f32)
    for ref, v in ((rx, r), (rc, s)):
        ref[16 * t : 16 * t + 8, :] = v[0:8, 0:NV]
        ref[16 * t + 8 : 16 * t + 16, :] = v[8:16, NV : 2 * NV]


def forces(xs, cs, rx, rc):
    def get(ref, k):
        return ref[pl.ds(k, 8, stride=8), :]

    inv = 1.0 / SQ
    q = get(rx, 6)
    r = get(rc, 6)
    react = [cs[k] * q - (get(rx, k) + get(rx, 3 + k)) * inv for k in range(3)]
    push = [xs[k] * r - (get(rc, k) + get(rc, 3 + k)) * inv for k in range(3)]
    return push, react


class Groups:
    def __init__(self, xg, vg, sg, lx, lc, rx, rc, eb, ab):
        self.r = (xg, vg, sg, lx, lc, rx, rc, eb, ab)

    def second(self, i, g, put):
        xg, vg, sg, lx, lc, rx, rc, eb, ab = self.r
        u, t = divmod(i, 4)
        e = [eb[u, t, k] for k in range(4)]
        sums(t, e, lx.at[u], lc.at[u], rx.at[u], rc.at[u])
        if t == 3:
            xs = [xg[u, c] for c in range(3)]
            cs = [vg[u, c] for c in range(3)]
            put(g, *forces(xs, cs, rx.at[u], rc.at[u]))

    def phase(self, base, count, load, put, before=None):
        xg, vg, sg, lx, lc, rx, rc, eb, ab = self.r
        for i in range(count * 4):
            u, t = divmod(i, 4)
            if t == 0:
                load(u, base + u)
                xs = [xg[u, c] for c in range(3)]
                vs = [vg[u, c] for c in range(3)]
                cs = prepare(xs, vs, sg[u], lx.at[u], lc.at[u], ab.at[u])
                for c in range(3):
                    vg[u, c] = cs[c]
            j = i - LAG
            if j >= 0:
                self.second(j, base + j // 4, put)
            elif before is not None:
                n, last, put_last = before
                self.second(n * 4 + j, last, put_last)
            high, low = energies(ab.at[u], t)
            eb[u, t, 0] = high[:, :NV]
            eb[u, t, 1] = low[:, :NV]
            eb[u, t, 2] = high[:, NV:]
            eb[u, t, 3] = low[:, NV:]
        return count, base + count - 1, put

    def flush(self, before):
        n, last, put = before
        for j in range(n * 4 - LAG, n * 4):
            self.second(j, last, put)

    def loop(self, total, count, load, put, after):
        def step(s, carry):
            base = s * count
            self.phase(base, count, load, put, (count, jnp.maximum(base - 1, 0), put))
            for u in range(count):
                after(base + u - 1)
            return carry

        lax.fori_loop(0, total // count, step, 0)
        self.flush((count, total - 1, put))
        after(total - 1)


def rows8(g):
    return pl.ds(pl.multiple_of(g * 8, 8), 8)


def pair_kernel(
    *refs,
):
    ins, refs = refs[:8], refs[8:]
    outs, refs = refs[:5], refs[5:]
    ret_b, ret_f, *refs = refs
    here, refs = refs[:8], refs[8:]
    rp, fp, loc, pick, fpick, rs, verts, stiff = here
    made, refs = refs[:5], refs[5:]
    push_l, react_l, react_b, react_f, meta = made
    got_b, got_f, out_b, out_f, back_b, back_f, brd, gv, *work, sems, fsems, isems, osems = refs
    xg, vg, sg = work[:3]
    me_t = lax.axis_index("slab")
    me_b = lax.axis_index("brick")
    moves = [pltpu.make_async_copy(a, b, isems.at[k]) for k, (a, b) in enumerate(zip(ins, here))]
    for move in moves:
        move.start()
    barrier = greet(me_t, me_b)
    for move in moves:
        move.wait()
    ask_b = Brick(out_b, got_b, sems.at[0], sems.at[1], me_t, me_b)
    ask_f = Face(out_f, got_f, fsems.at[0], fsems.at[1], me_t, me_b)
    give_b = Brick(back_b, ret_b, sems.at[2], sems.at[3], me_t, me_b)
    give_f = Face(back_f, ret_f, fsems.at[2], fsems.at[3], me_t, me_b)

    def row(c, idx):
        return jnp.where(idx >= 0, verts[c, pl.ds(jnp.maximum(idx, 0), 1), :], FAR)

    for s in range(NB):
        out_b[s, 3] = jnp.broadcast_to(rs[:, s : s + 1].astype(f32), (NS, NV))
    got_b[me_b, 0:3] = jnp.full((3, NS, NV), FAR, f32)
    got_b[me_b, 3] = jnp.zeros((NS, NV), f32)

    @pl.when(me_t == 0)
    def _():
        got_f[0] = jnp.full((3, NF, NV), FAR, f32)

    @pl.when(me_t == 3)
    def _():
        got_f[1] = jnp.full((3, NF, NV), FAR, f32)

    groups = Groups(*work)
    half = NF // 8

    def pushing(u, p, idx):
        for c in range(3):
            vg[u, c, p : p + 1, :] = verts[c, pl.ds(idx, 1), :]
        sg[u, p : p + 1, :] = stiff[pl.ds(idx, 1), :]

    def load_local(u, g):
        for p in range(8):
            a = loc[0, g * 8 + p]
            for c in range(3):
                xg[u, c, p : p + 1, :] = verts[c, pl.ds(a, 1), :]
            pushing(u, p, loc[1, g * 8 + p])

    def load_first(u, g):
        load_local(u, g)
        for h in range(2):
            s = 2 * g + h
            for k in range(NS):
                for c in range(3):
                    out_b[s, c, k : k + 1, :] = row(c, rp[k, s])
        side = g // half
        for k in range(8):
            j = lax.rem(g, half) * 8 + k
            for c in range(3):
                out_f[side, c, pl.ds(j, 1), :] = row(c, fp[side, j])

    def load_second(u, g):
        load_local(u, g)
        for k in range(16):
            j = (g - FIRST) * 16 + k
            idx = pick[0, j]
            for c in range(3):
                brd[c, pl.ds(j, 1), :] = verts[c, pl.ds(idx, 1), :]
            brd[3, pl.ds(j, 1), :] = stiff[pl.ds(idx, 1), :]

    def put_local(g, push, re):
        for c in range(3):
            push_l[c, rows8(g), :] = push[c]
            react_l[c, rows8(g), :] = re[c]

    tail = groups.phase(0, FIRST, load_first, put_local)
    greeted(barrier, me_t)
    ask_f.start()
    ask_b.start()
    tail = groups.phase(FIRST, SECOND, load_second, put_local, tail)
    copies = []

    def give_out(k):
        copies.append(pltpu.make_async_copy(made[k], outs[k], osems.at[k]))
        copies[-1].start()

    def load_face(u, g):
        side = g // half
        k = lax.rem(g, half)
        for c in range(3):
            xg[u, c] = got_f[side, c, rows8(k), :]
        for p in range(8):
            pushing(u, p, fpick[side, k * 8 + p])

    def put_face(g, push, re):
        side = g // half
        k = lax.rem(g, half)
        for c in range(3):
            back_f[side, c, rows8(k), :] = push[c]
            react_f[c, rows8(g), :] = re[c]

    ask_f.wait()
    groups.flush(groups.phase(0, 2 * half, load_face, put_face, tail))
    give_f.start()
    give_out(3)
    ends = [pltpu.make_async_copy(back_f.at[k], ret_f.at[k], fsems.at[4, k]) for k in range(2)]
    for side in range(2):

        @pl.when(jnp.logical_not(give_f.there(side)))
        def _(side=side):
            ends[side].start()

    ask_b.wait()
    table = jnp.concatenate([brd[c] for c in range(4)], 1)
    t1 = table.astype(bf16)
    r = table - t1.astype(f32)
    t2 = r.astype(bf16)
    t3 = (r - t2.astype(f32)).astype(bf16)
    parts = jnp.concatenate([t1, t2, t3], 0)
    lane = lax.broadcasted_iota(i32, (NV, NV), 1).astype(f32)
    for h in range(NBS // NV):
        want = jnp.concatenate([got_b[h * 16 + s, 3] for s in range(16)], 0)
        for s in range(16):
            meta[h * 16 + s] = got_b[h * 16 + s, 3]
        hot = jnp.where(want == lane, 1.0, 0.0).astype(bf16)
        v = jnp.dot(jnp.concatenate([hot] * 3, 1), parts, preferred_element_type=f32)
        for c in range(4):
            gv[c, h * NV : (h + 1) * NV, :] = v[:, c * NV : (c + 1) * NV]

    give_out(4)

    def load_brick(u, o):
        s = lax.rem(me_b + o, NB)
        for c in range(3):
            xg[u, c] = got_b[s, c]
            vg[u, c] = gv[c, rows8(s), :]
        sg[u] = gv[3, rows8(s), :]

    def put_brick(o, push, re):
        s = lax.rem(me_b + o, NB)
        for c in range(3):
            back_b[s, c] = push[c]
            react_b[c, rows8(s), :] = re[c]

    def send_back(o):
        @pl.when(o >= 1)
        def _():
            give_b.copy(o).start()

    groups.loop(NB, U, load_brick, put_brick, send_back)
    give_out(2)
    own = pltpu.make_async_copy(back_b.at[me_b], ret_b.at[me_b], osems.at[5])
    own.start()
    late = FIRST + SECOND
    groups.flush(groups.phase(late, NL // 8 - late, load_local, put_local))
    give_out(0)
    give_out(1)
    give_b.wait()
    give_f.wait()
    for side in range(2):

        @pl.when(jnp.logical_not(give_f.there(side)))
        def _(side=side):
            ends[side].wait()

    own.wait()
    for copy in copies:
        copy.wait()


MADE = ((3, NL, NV), (3, NL, NV), (3, NBS, NV), (3, 2 * NF, NV), (NB, NS, NV))
BACK = ((NB, 3, NS, NV), (2, 3, NF, NV))


def pairs(rp, fp, loc, pick, fpick, rs, verts, stiff):
    sds = jax.ShapeDtypeStruct
    return pl.pallas_call(
        pair_kernel,
        name="pairs",
        out_shape=tuple(sds(shape, f32) for shape in MADE + BACK),
        in_specs=[hbm] * 8,
        out_specs=(hbm,) * 7,
        scratch_shapes=[
            *[pltpu.SMEM(shape, i32) for shape in LISTS],
            pltpu.VMEM((NS, NB), i32),
            pltpu.VMEM((3, NP, NV), f32),
            pltpu.VMEM((NP, NV), f32),
            *[pltpu.VMEM(shape, f32) for shape in MADE],
            pltpu.VMEM((NB, 4, NS, NV), f32),
            pltpu.VMEM((2, 3, NF, NV), f32),
            pltpu.VMEM((NB, 4, NS, NV), f32),
            pltpu.VMEM((2, 3, NF, NV), f32),
            pltpu.VMEM((NB, 3, NS, NV), f32),
            pltpu.VMEM((2, 3, NF, NV), f32),
            pltpu.VMEM((4, NV, NV), f32),
            pltpu.VMEM((4, NBS, NV), f32),
            pltpu.VMEM((U, 3, 8, NV), f32),
            pltpu.VMEM((U, 3, 8, NV), f32),
            pltpu.VMEM((U, 8, NV), f32),
            *[pltpu.VMEM((U, 64, NV), f32)] * 4,
            pltpu.VMEM((U, 4, 4, NV, NV), bf16),
            pltpu.VMEM((U, 2, NV, NV), f32),
            pltpu.SemaphoreType.DMA((4, NB)),
            pltpu.SemaphoreType.DMA((5, 2)),
            pltpu.SemaphoreType.DMA((8,)),
            pltpu.SemaphoreType.DMA((6,)),
        ],
        compiler_params=pltpu.CompilerParams(collective_id=0, has_side_effects=True),
    )(rp, fp, loc, pick, fpick, rs, verts, stiff)


def flat(a):
    lane = lax.broadcasted_iota(i32, (NB, NBS), 1)
    wide = (lane // NS == lax.broadcasted_iota(i32, (NB, NBS), 0)).astype(f32).astype(bf16)
    high, low = split(a.astype(f32))
    row = jnp.dot(high.astype(bf16), wide, preferred_element_type=f32)
    row = row + jnp.dot(low.astype(bf16), wide, preferred_element_type=f32)
    own = lax.broadcasted_iota(i32, (NS, NBS), 0) == lax.broadcasted_iota(i32, (NS, NBS), 1) % NS
    return jnp.sum(jnp.where(own, row, 0.0), axis=0, keepdims=True)


def two(x):
    high, low = split(x)
    return high.astype(bf16), low.astype(bf16)


def side_by_side(a):
    return jnp.concatenate([a[0:1], a[1:2]], 1).astype(f32)


def merge_kernel(*refs):
    n_in = 5 + len(MADE) + len(BACK)
    ins, out, here, refs = refs[:n_in], refs[n_in], refs[n_in + 1 : 2 * n_in + 1], refs[2 * n_in + 1 :]
    rp, fp, loc, pick, fpick, push_l, react_l, react_b, react_f, meta, ret_b, ret_f = here
    made, isems, osems = refs
    moves = [pltpu.make_async_copy(a, b, isems.at[k]) for k, (a, b) in enumerate(zip(ins, here))]
    order = [9, 7, 0, 1, 2, 3, 4, 5, 6, 8, 10, 11]
    for k in order:
        moves[k].start()
    for k in order[:2]:
        moves[k].wait()
    cat = jnp.concatenate

    def lanes(ref):
        return cat([ref[c] for c in range(3)], 1)

    lane = lax.broadcasted_iota(i32, (NV, NV), 1).astype(f32)
    hots = []
    for h in range(NBS // NV):
        want = cat([meta[h * 16 + s] for s in range(16)], 0)
        hots.append(jnp.where(want == lane, 1.0, 0.0).astype(bf16))
    hot = cat(hots, 0)
    border = lax.dot_general(cat([hot] * 2, 0), cat(two(lanes(react_b)), 0), D0, preferred_element_type=f32)
    for k in order[2:7]:
        moves[k].wait()
    pushed = cat([loc[0:1].astype(f32), flat(rp[...]), side_by_side(fp[...])], 1)
    pushing = cat([loc[1:2].astype(f32), pick[...].astype(f32), side_by_side(fpick[...])], 1)
    for k in order[7:]:
        moves[k].wait()

    back_b = cat([cat([ret_b[s, c] for s in range(NB)], 0) for c in range(3)], 1)
    back_f = cat([cat([ret_f[k, c] for k in range(2)], 0) for c in range(3)], 1)
    push = cat(two(cat([lanes(push_l), back_b, back_f], 0)), 0)
    react = cat(two(cat([lanes(react_l), border, lanes(react_f)], 0)), 0)

    size = NP // CHUNKS
    copies = []
    for n in range(CHUNKS):

        def scatter(idx, values):
            row = lax.broadcasted_iota(i32, (size, idx.shape[1]), 0).astype(f32) + float(n * size)
            one = jnp.where(row == idx, 1.0, 0.0).astype(bf16)
            return jnp.dot(cat([one, one], 1), values, preferred_element_type=f32)

        p = scatter(pushed, push)
        q = scatter(pushing, react)
        rows = pl.ds(n * size, size)
        for c in range(3):
            r = q[:, c * NV : (c + 1) * NV]
            s = r + pltpu.roll(r, 1, 1) + pltpu.roll(r, 2, 1)
            made[c, rows, :] = p[:, c * NV : (c + 1) * NV] + s * (1.0 / 3.0)
        copies.append(pltpu.make_async_copy(made.at[:, rows, :], out.at[:, rows, :], osems.at[n]))
        copies[-1].start()
    for copy in copies:
        copy.wait()


def merge(*args):
    return pl.pallas_call(
        merge_kernel,
        name="merge",
        out_shape=jax.ShapeDtypeStruct((3, NP, NV), f32),
        in_specs=[hbm] * len(args),
        out_specs=hbm,
        scratch_shapes=[
            *[pltpu.VMEM(shape, i32) for shape in LISTS],
            *[pltpu.VMEM(shape, f32) for shape in MADE + BACK],
            pltpu.VMEM((3, NP, NV), f32),
            pltpu.SemaphoreType.DMA((len(args),)),
            pltpu.SemaphoreType.DMA((CHUNKS,)),
        ],
    )(*args)


def body(verts, stiffness, local_pairs, border_pick, recv_src, recv_pair, face_pick, face_pair):
    rp = recv_pair[0].T
    lists = (rp, face_pair[0], local_pairs[0], border_pick, face_pick[0])
    made = pairs(*lists, recv_src[0].T, verts.transpose(1, 0, 2), stiffness)
    return merge(*lists, *made).transpose(1, 0, 2)


def solution(mesh):
    both = ("slab", "brick")
    placed = (
        P(both, None, None),
        P(both, None),
        P(both, None, None),
        P(both, None),
        P(both, None, None),
        P(both, None, None),
        P(both, None, None),
        P(both, None, None),
    )
    return jax.shard_map(
        body, mesh=mesh, in_specs=placed, out_specs=P(both, None, None), check_vma=False
    )
```

```python
import math

import jax
import jax.numpy as jnp
from jax import lax
from jax.experimental import pallas as pl
from jax.experimental.pallas import tpu as pltpu
from jax.sharding import PartitionSpec as P

f32 = jnp.float32
bf16 = jnp.bfloat16
i32 = jnp.int32
MESH = pl.DeviceIdType.MESH

NP = 1024
NV = 128
NB = 32
NS = 8
NF = 64
NBS = NB * NS
NL = 256
FIRST = 16
SECOND = 4
SQ = math.sqrt(math.log2(math.e))
FAR = 1.0e4
U = 16
CHUNKS = 4
LAG = 4
DN = (((1,), (1,)), ((), ()))
D0 = (((0,), (0,)), ((), ()))

vm = pl.BlockSpec(memory_space=pltpu.VMEM)
hbm = pl.BlockSpec(memory_space=pltpu.HBM)
LISTS = ((NS, NB), (2, NF), (2, NL), (1, NV), (2, NF))


def greet(me_t, me_b):
    sem = pltpu.get_barrier_semaphore()

    def one(o, c):
        pl.semaphore_signal(
            sem, inc=1, device_id=(me_t, lax.rem(me_b + o, NB)), device_id_type=MESH
        )
        return c

    lax.fori_loop(1, NB, one, 0)

    @pl.when(me_t > 0)
    def _():
        pl.semaphore_signal(sem, inc=1, device_id=(me_t - 1, me_b), device_id_type=MESH)

    @pl.when(me_t < 3)
    def _():
        pl.semaphore_signal(sem, inc=1, device_id=(me_t + 1, me_b), device_id_type=MESH)

    return sem


def greeted(sem, me_t):
    faces = (me_t > 0).astype(i32) + (me_t < 3).astype(i32)
    pl.semaphore_wait(sem, NB - 1 + faces)


class Brick:
    def __init__(self, src, dst, s_sem, r_sem, me_t, me_b):
        self.a = (src, dst, s_sem, r_sem, me_t, me_b)

    def copy(self, o):
        src, dst, s_sem, r_sem, me_t, me_b = self.a
        peer = lax.rem(me_b + o, NB)
        return pltpu.make_async_remote_copy(
            src_ref=src.at[peer],
            dst_ref=dst.at[me_b],
            send_sem=s_sem,
            recv_sem=r_sem,
            device_id=(me_t, peer),
            device_id_type=MESH,
        )

    def start(self):
        def one(o, c):
            self.copy(o).start()
            return c

        lax.fori_loop(1, NB, one, 0)

    def all(self):
        src, dst, s_sem, r_sem, me_t, me_b = self.a
        rest = pl.ds(0, NB - 1)
        return pltpu.make_async_remote_copy(
            src_ref=src.at[rest],
            dst_ref=dst.at[rest],
            send_sem=s_sem,
            recv_sem=r_sem,
            device_id=(me_t, lax.rem(me_b + 1, NB)),
            device_id_type=MESH,
        )

    def wait_recv(self):
        self.all().wait_recv()

    def wait_send(self):
        self.all().wait_send()


class Face:
    def __init__(self, src, dst, s_sem, r_sem, me_t, me_b):
        self.a = (src, dst, s_sem, r_sem, me_t, me_b)

    def copy(self, side, arrival=False):
        src, dst, s_sem, r_sem, me_t, me_b = self.a
        at = side if arrival else 1 - side
        return pltpu.make_async_remote_copy(
            src_ref=src.at[side],
            dst_ref=dst.at[at],
            send_sem=s_sem.at[side],
            recv_sem=r_sem.at[at],
            device_id=(me_t + (1 if side else -1), me_b),
            device_id_type=MESH,
        )

    def there(self, side):
        return (self.a[4] < 3) if side else (self.a[4] > 0)

    def start(self):
        for side in range(2):

            @pl.when(self.there(side))
            def _(side=side):
                self.copy(side).start()

    def wait(self):
        for side in range(2):

            @pl.when(self.there(side))
            def _(side=side):
                self.copy(side, True).wait_recv()
                self.copy(side).wait_send()


def split(x):
    high = x.astype(bf16).astype(f32)
    return high, x - high


def ahead(v, k):
    return pltpu.roll(v, NV - k, 1)


def prepare(xs, vs, stiff, lx, lc, ab):
    one = jnp.ones((8, NV), f32)
    zero = jnp.zeros((8, NV), f32)
    cs = [(v + ahead(v, 1) + ahead(v, 2)) * (1.0 / 3.0) for v in vs]
    xp = [x * SQ for x in xs]
    cp = [c * SQ for c in cs]
    x1, x2 = zip(*[split(x) for x in xp])
    c1, c2 = zip(*[split(c) for c in cp])
    n = -0.5 * (xp[0] * xp[0] + xp[1] * xp[1] + xp[2] * xp[2])
    m = -0.5 * (cp[0] * cp[0] + cp[1] * cp[1] + cp[2] * cp[2]) + jnp.log2(stiff) - 7.0
    n1, r = split(n)
    n2, n3 = split(r)
    m1, r = split(m)
    m2, m3 = split(r)
    for k, r in enumerate([*x1, *x1, *x2, n1, n2, n3, one, one, one, zero]):
        ab[0, 8 * k : 8 * k + 8, :] = r
    for k, r in enumerate([*c1, *c2, *c1, one, one, one, m1, m2, m3, zero]):
        ab[1, 8 * k : 8 * k + 8, :] = r
    for ref, rows in ((lx, [*x1, *x2, one, zero]), (lc, [*c1, *c2, one, zero])):
        for k, r in enumerate(rows):
            ref[pl.ds(k, 8, stride=8), :] = r
    return cs


def energies(ab, t):
    def get(side, p):
        return ab[side, pl.ds(p, 16, stride=8), :].astype(bf16)

    cat = jnp.concatenate
    a = cat([get(0, 2 * t), get(0, 2 * t + 1)], 0).T
    b0 = get(1, 2 * t)
    b1 = get(1, 2 * t + 1)
    zero = jnp.zeros_like(b0)
    b = cat([cat([b0, zero], 1), cat([zero, b1], 1)], 0)
    e = jnp.exp2(jnp.dot(a, b, preferred_element_type=f32))
    high = e.astype(bf16)
    return high, (e - high.astype(f32)).astype(bf16)


def sums(t, e, lx, lc, rx, rc):
    h0, l0, h1, l1 = e
    rows = slice(16 * t, 16 * t + 16)
    x = lx[rows, :].astype(bf16)
    c = lc[rows, :].astype(bf16)
    cat = jnp.concatenate
    e_ij = cat([cat([h0, h1], 1), cat([l0, l1], 1)], 0)
    e_ji = cat([cat([h0, l0], 1), cat([h1, l1], 1)], 0)
    r = jnp.dot(cat([x, x], 1), e_ij, preferred_element_type=f32)
    s = lax.dot_general(cat([c, c], 1), e_ji, DN, preferred_element_type=f32)
    for ref, v in ((rx, r), (rc, s)):
        ref[16 * t : 16 * t + 8, :] = v[0:8, 0:NV]
        ref[16 * t + 8 : 16 * t + 16, :] = v[8:16, NV : 2 * NV]


def forces(xs, cs, rx, rc):
    def get(ref, k):
        return ref[pl.ds(k, 8, stride=8), :]

    inv = 1.0 / SQ
    q = get(rx, 6)
    r = get(rc, 6)
    react = [cs[k] * q - (get(rx, k) + get(rx, 3 + k)) * inv for k in range(3)]
    push = [xs[k] * r - (get(rc, k) + get(rc, 3 + k)) * inv for k in range(3)]
    return push, react


class Groups:
    def __init__(self, xg, vg, sg, lx, lc, rx, rc, eb, ab):
        self.r = (xg, vg, sg, lx, lc, rx, rc, eb, ab)

    def second(self, i, g, put):
        xg, vg, sg, lx, lc, rx, rc, eb, ab = self.r
        u, t = divmod(i, 4)
        e = [eb[u, t, k] for k in range(4)]
        sums(t, e, lx.at[u], lc.at[u], rx.at[u], rc.at[u])
        if t == 3:
            xs = [xg[u, c] for c in range(3)]
            cs = [vg[u, c] for c in range(3)]
            put(g, *forces(xs, cs, rx.at[u], rc.at[u]))

    def phase(self, base, count, load, put, before=None):
        xg, vg, sg, lx, lc, rx, rc, eb, ab = self.r
        for i in range(count * 4):
            u, t = divmod(i, 4)
            if t == 0:
                load(u, base + u)
                xs = [xg[u, c] for c in range(3)]
                vs = [vg[u, c] for c in range(3)]
                cs = prepare(xs, vs, sg[u], lx.at[u], lc.at[u], ab.at[u])
                for c in range(3):
                    vg[u, c] = cs[c]
            j = i - LAG
            if j >= 0:
                self.second(j, base + j // 4, put)
            elif before is not None:
                n, last, put_last = before
                self.second(n * 4 + j, last, put_last)
            high, low = energies(ab.at[u], t)
            eb[u, t, 0] = high[:, :NV]
            eb[u, t, 1] = low[:, :NV]
            eb[u, t, 2] = high[:, NV:]
            eb[u, t, 3] = low[:, NV:]
        return count, base + count - 1, put

    def flush(self, before):
        n, last, put = before
        for j in range(n * 4 - LAG, n * 4):
            self.second(j, last, put)

    def loop(self, total, count, load, put, after):
        def step(s, carry):
            base = s * count
            self.phase(base, count, load, put, (count, jnp.maximum(base - 1, 0), put))
            for u in range(count):
                after(base + u - 1)
            return carry

        lax.fori_loop(0, total // count, step, 0)
        self.flush((count, total - 1, put))
        after(total - 1)


def rows8(g):
    return pl.ds(pl.multiple_of(g * 8, 8), 8)


def pair_kernel(
    *refs,
):
    ins, refs = refs[:8], refs[8:]
    outs, refs = refs[:5], refs[5:]
    ret_b, ret_f, *refs = refs
    here, refs = refs[:8], refs[8:]
    rp, fp, loc, pick, fpick, rs, verts, stiff = here
    made, refs = refs[:5], refs[5:]
    push_l, react_l, react_b, react_f, meta = made
    got_b, got_f, out_b, out_f, back_b, back_f, brd, gv, *work, sems, fsems, isems, osems = refs
    xg, vg, sg = work[:3]
    me_t = lax.axis_index("slab")
    me_b = lax.axis_index("brick")
    moves = [pltpu.make_async_copy(a, b, isems.at[k]) for k, (a, b) in enumerate(zip(ins, here))]
    for move in moves:
        move.start()
    barrier = greet(me_t, me_b)
    for move in moves:
        move.wait()
    ask_b = Brick(out_b, got_b, sems.at[0], sems.at[1], me_t, me_b)
    ask_f = Face(out_f, got_f, fsems.at[0], fsems.at[1], me_t, me_b)
    give_b = Brick(back_b, ret_b, sems.at[2], sems.at[3], me_t, me_b)
    give_f = Face(back_f, ret_f, fsems.at[2], fsems.at[3], me_t, me_b)

    def row(c, idx):
        return jnp.where(idx >= 0, verts[c, pl.ds(jnp.maximum(idx, 0), 1), :], FAR)

    for s in range(NB):
        out_b[s, 3] = jnp.broadcast_to(rs[:, s : s + 1].astype(f32), (NS, NV))
    got_b[me_b, 0:3] = jnp.full((3, NS, NV), FAR, f32)
    got_b[me_b, 3] = jnp.zeros((NS, NV), f32)

    @pl.when(me_t == 0)
    def _():
        got_f[0] = jnp.full((3, NF, NV), FAR, f32)

    @pl.when(me_t == 3)
    def _():
        got_f[1] = jnp.full((3, NF, NV), FAR, f32)

    groups = Groups(*work)
    half = NF // 8

    def pushing(u, p, idx):
        for c in range(3):
            vg[u, c, p : p + 1, :] = verts[c, pl.ds(idx, 1), :]
        sg[u, p : p + 1, :] = stiff[pl.ds(idx, 1), :]

    def load_local(u, g):
        for p in range(8):
            a = loc[0, g * 8 + p]
            for c in range(3):
                xg[u, c, p : p + 1, :] = verts[c, pl.ds(a, 1), :]
            pushing(u, p, loc[1, g * 8 + p])

    def load_first(u, g):
        load_local(u, g)
        for h in range(2):
            s = 2 * g + h
            for k in range(NS):
                for c in range(3):
                    out_b[s, c, k : k + 1, :] = row(c, rp[k, s])
        side = g // half
        for k in range(8):
            j = lax.rem(g, half) * 8 + k
            for c in range(3):
                out_f[side, c, pl.ds(j, 1), :] = row(c, fp[side, j])

    def put_local(g, push, re):
        for c in range(3):
            push_l[c, rows8(g), :] = push[c]
            react_l[c, rows8(g), :] = re[c]

    tail = groups.phase(0, FIRST, load_first, put_local)
    greeted(barrier, me_t)
    ask_f.start()
    ask_b.start()
    tail = groups.phase(FIRST, SECOND, load_local, put_local, tail)
    copies = []

    def give_out(k):
        copies.append(pltpu.make_async_copy(made[k], outs[k], osems.at[k]))
        copies[-1].start()

    def load_face(u, g):
        side = g // half
        k = lax.rem(g, half)
        for c in range(3):
            xg[u, c] = got_f[side, c, rows8(k), :]
        for p in range(8):
            pushing(u, p, fpick[side, k * 8 + p])
            j = g * 8 + p
            idx = pick[0, j]
            for c in range(3):
                brd[c, pl.ds(j, 1), :] = verts[c, pl.ds(idx, 1), :]
            brd[3, pl.ds(j, 1), :] = stiff[pl.ds(idx, 1), :]

    def put_face(g, push, re):
        side = g // half
        k = lax.rem(g, half)
        for c in range(3):
            back_f[side, c, rows8(k), :] = push[c]
            react_f[c, rows8(g), :] = re[c]

    ask_f.wait()
    groups.flush(groups.phase(0, 2 * half, load_face, put_face, tail))
    give_f.start()
    give_out(3)
    ends = [pltpu.make_async_copy(back_f.at[k], ret_f.at[k], fsems.at[4, k]) for k in range(2)]
    for side in range(2):

        @pl.when(jnp.logical_not(give_f.there(side)))
        def _(side=side):
            ends[side].start()

    ask_b.wait_recv()
    table = jnp.concatenate([brd[c] for c in range(4)], 1)
    t1 = table.astype(bf16)
    r = table - t1.astype(f32)
    t2 = r.astype(bf16)
    t3 = (r - t2.astype(f32)).astype(bf16)
    parts = jnp.concatenate([t1, t2, t3], 0)
    lane = lax.broadcasted_iota(i32, (NV, NV), 1).astype(f32)
    for h in range(NBS // NV):
        want = jnp.concatenate([got_b[h * 16 + s, 3] for s in range(16)], 0)
        for s in range(16):
            meta[h * 16 + s] = got_b[h * 16 + s, 3]
        hot = jnp.where(want == lane, 1.0, 0.0).astype(bf16)
        v = jnp.dot(jnp.concatenate([hot] * 3, 1), parts, preferred_element_type=f32)
        for c in range(4):
            gv[c, h * NV : (h + 1) * NV, :] = v[:, c * NV : (c + 1) * NV]

    give_out(4)

    def load_brick(u, o):
        s = lax.rem(me_b + o, NB)
        for c in range(3):
            xg[u, c] = got_b[s, c]
            vg[u, c] = gv[c, rows8(s), :]
        sg[u] = gv[3, rows8(s), :]

    def put_brick(o, push, re):
        s = lax.rem(me_b + o, NB)
        for c in range(3):
            back_b[s, c] = push[c]
            react_b[c, rows8(s), :] = re[c]

    def send_back(o):
        @pl.when(o >= 1)
        def _():
            give_b.copy(o).start()

    groups.loop(NB, U, load_brick, put_brick, send_back)
    give_out(2)
    own = pltpu.make_async_copy(back_b.at[me_b], ret_b.at[me_b], osems.at[5])
    own.start()
    late = FIRST + SECOND
    groups.flush(groups.phase(late, NL // 8 - late, load_local, put_local))
    give_out(0)
    give_out(1)
    ask_b.wait_send()
    give_b.wait_recv()
    give_b.wait_send()
    give_f.wait()
    for side in range(2):

        @pl.when(jnp.logical_not(give_f.there(side)))
        def _(side=side):
            ends[side].wait()

    own.wait()
    for copy in copies:
        copy.wait()


MADE = ((3, NL, NV), (3, NL, NV), (3, NBS, NV), (3, 2 * NF, NV), (NB, NS, NV))
BACK = ((NB, 3, NS, NV), (2, 3, NF, NV))


def pairs(rp, fp, loc, pick, fpick, rs, verts, stiff):
    sds = jax.ShapeDtypeStruct
    return pl.pallas_call(
        pair_kernel,
        name="pairs",
        out_shape=tuple(sds(shape, f32) for shape in MADE + BACK),
        in_specs=[hbm] * 8,
        out_specs=(hbm,) * 7,
        scratch_shapes=[
            *[pltpu.SMEM(shape, i32) for shape in LISTS],
            pltpu.VMEM((NS, NB), i32),
            pltpu.VMEM((3, NP, NV), f32),
            pltpu.VMEM((NP, NV), f32),
            *[pltpu.VMEM(shape, f32) for shape in MADE],
            pltpu.VMEM((NB, 4, NS, NV), f32),
            pltpu.VMEM((2, 3, NF, NV), f32),
            pltpu.VMEM((NB, 4, NS, NV), f32),
            pltpu.VMEM((2, 3, NF, NV), f32),
            pltpu.VMEM((NB, 3, NS, NV), f32),
            pltpu.VMEM((2, 3, NF, NV), f32),
            pltpu.VMEM((4, NV, NV), f32),
            pltpu.VMEM((4, NBS, NV), f32),
            pltpu.VMEM((U, 3, 8, NV), f32),
            pltpu.VMEM((U, 3, 8, NV), f32),
            pltpu.VMEM((U, 8, NV), f32),
            *[pltpu.VMEM((U, 64, NV), f32)] * 4,
            pltpu.VMEM((U, 4, 4, NV, NV), bf16),
            pltpu.VMEM((U, 2, NV, NV), f32),
            pltpu.SemaphoreType.DMA((4,)),
            pltpu.SemaphoreType.DMA((5, 2)),
            pltpu.SemaphoreType.DMA((8,)),
            pltpu.SemaphoreType.DMA((6,)),
        ],
        compiler_params=pltpu.CompilerParams(collective_id=0, has_side_effects=True),
    )(rp, fp, loc, pick, fpick, rs, verts, stiff)


def flat(a):
    lane = lax.broadcasted_iota(i32, (NB, NBS), 1)
    wide = (lane // NS == lax.broadcasted_iota(i32, (NB, NBS), 0)).astype(f32).astype(bf16)
    high, low = split(a.astype(f32))
    row = jnp.dot(high.astype(bf16), wide, preferred_element_type=f32)
    row = row + jnp.dot(low.astype(bf16), wide, preferred_element_type=f32)
    own = lax.broadcasted_iota(i32, (NS, NBS), 0) == lax.broadcasted_iota(i32, (NS, NBS), 1) % NS
    return jnp.sum(jnp.where(own, row, 0.0), axis=0, keepdims=True)


def two(x):
    high, low = split(x)
    return high.astype(bf16), low.astype(bf16)


def side_by_side(a):
    return jnp.concatenate([a[0:1], a[1:2]], 1).astype(f32)


def merge_kernel(*refs):
    n_in = 5 + len(MADE) + len(BACK)
    ins, out, here, refs = refs[:n_in], refs[n_in], refs[n_in + 1 : 2 * n_in + 1], refs[2 * n_in + 1 :]
    rp, fp, loc, pick, fpick, push_l, react_l, react_b, react_f, meta, ret_b, ret_f = here
    made, isems, osems = refs
    moves = [pltpu.make_async_copy(a, b, isems.at[k]) for k, (a, b) in enumerate(zip(ins, here))]
    order = [9, 7, 0, 1, 2, 3, 4, 5, 6, 8, 10, 11]
    for k in order:
        moves[k].start()
    for k in order[:2]:
        moves[k].wait()
    cat = jnp.concatenate

    def lanes(ref):
        return cat([ref[c] for c in range(3)], 1)

    lane = lax.broadcasted_iota(i32, (NV, NV), 1).astype(f32)
    hots = []
    for h in range(NBS // NV):
        want = cat([meta[h * 16 + s] for s in range(16)], 0)
        hots.append(jnp.where(want == lane, 1.0, 0.0).astype(bf16))
    hot = cat(hots, 0)
    border = lax.dot_general(cat([hot] * 2, 0), cat(two(lanes(react_b)), 0), D0, preferred_element_type=f32)
    for k in order[2:7]:
        moves[k].wait()
    pushed = cat([loc[0:1].astype(f32), flat(rp[...]), side_by_side(fp[...])], 1)
    pushing = cat([loc[1:2].astype(f32), pick[...].astype(f32), side_by_side(fpick[...])], 1)
    for k in order[7:]:
        moves[k].wait()

    back_b = cat([cat([ret_b[s, c] for s in range(NB)], 0) for c in range(3)], 1)
    back_f = cat([cat([ret_f[k, c] for k in range(2)], 0) for c in range(3)], 1)
    push = cat(two(cat([lanes(push_l), back_b, back_f], 0)), 0)
    react = cat(two(cat([lanes(react_l), border, lanes(react_f)], 0)), 0)

    size = NP // CHUNKS
    copies = []
    for n in range(CHUNKS):

        def scatter(idx, values):
            row = lax.broadcasted_iota(i32, (size, idx.shape[1]), 0).astype(f32) + float(n * size)
            one = jnp.where(row == idx, 1.0, 0.0).astype(bf16)
            return jnp.dot(cat([one, one], 1), values, preferred_element_type=f32)

        p = scatter(pushed, push)
        q = scatter(pushing, react)
        rows = pl.ds(n * size, size)
        for c in range(3):
            r = q[:, c * NV : (c + 1) * NV]
            s = r + pltpu.roll(r, 1, 1) + pltpu.roll(r, 2, 1)
            made[c, rows, :] = p[:, c * NV : (c + 1) * NV] + s * (1.0 / 3.0)
        copies.append(pltpu.make_async_copy(made.at[:, rows, :], out.at[:, rows, :], osems.at[n]))
        copies[-1].start()
    for copy in copies:
        copy.wait()


def merge(*args):
    return pl.pallas_call(
        merge_kernel,
        name="merge",
        out_shape=jax.ShapeDtypeStruct((3, NP, NV), f32),
        in_specs=[hbm] * len(args),
        out_specs=hbm,
        scratch_shapes=[
            *[pltpu.VMEM(shape, i32) for shape in LISTS],
            *[pltpu.VMEM(shape, f32) for shape in MADE + BACK],
            pltpu.VMEM((3, NP, NV), f32),
            pltpu.SemaphoreType.DMA((len(args),)),
            pltpu.SemaphoreType.DMA((CHUNKS,)),
        ],
    )(*args)


def body(verts, stiffness, local_pairs, border_pick, recv_src, recv_pair, face_pick, face_pair):
    rp = recv_pair[0].T
    lists = (rp, face_pair[0], local_pairs[0], border_pick, face_pick[0])
    made = pairs(*lists, recv_src[0].T, verts.transpose(1, 0, 2), stiffness)
    return merge(*lists, *made).transpose(1, 0, 2)


def solution(mesh):
    both = ("slab", "brick")
    placed = (
        P(both, None, None),
        P(both, None),
        P(both, None, None),
        P(both, None),
        P(both, None, None),
        P(both, None, None),
        P(both, None, None),
        P(both, None, None),
    )
    return jax.shard_map(
        body, mesh=mesh, in_specs=placed, out_specs=P(both, None, None), check_vma=False
    )
```

```python
import math

import jax
import jax.numpy as jnp
from jax import lax
from jax.experimental import pallas as pl
from jax.experimental.pallas import tpu as pltpu
from jax.sharding import PartitionSpec as P

f32 = jnp.float32
bf16 = jnp.bfloat16
i32 = jnp.int32
MESH = pl.DeviceIdType.MESH

NP = 1024
NV = 128
NB = 32
NS = 8
NF = 64
NBS = NB * NS
NL = 256
FIRST = 16
SECOND = 4
SQ = math.sqrt(math.log2(math.e))
FAR = 1.0e4
U = 16
CHUNKS = 4
LAG = 4
DN = (((1,), (1,)), ((), ()))
D0 = (((0,), (0,)), ((), ()))

vm = pl.BlockSpec(memory_space=pltpu.VMEM)
hbm = pl.BlockSpec(memory_space=pltpu.HBM)
LISTS = ((NS, NB), (2, NF), (2, NL), (1, NV), (2, NF))


def greet(me_t, me_b):
    sem = pltpu.get_barrier_semaphore()

    def one(o, c):
        pl.semaphore_signal(
            sem, inc=1, device_id=(me_t, lax.rem(me_b + o, NB)), device_id_type=MESH
        )
        return c

    lax.fori_loop(1, NB, one, 0)

    @pl.when(me_t > 0)
    def _():
        pl.semaphore_signal(sem, inc=1, device_id=(me_t - 1, me_b), device_id_type=MESH)

    @pl.when(me_t < 3)
    def _():
        pl.semaphore_signal(sem, inc=1, device_id=(me_t + 1, me_b), device_id_type=MESH)

    return sem


def greeted(sem, me_t):
    faces = (me_t > 0).astype(i32) + (me_t < 3).astype(i32)
    pl.semaphore_wait(sem, NB - 1 + faces)


class Brick:
    def __init__(self, src, dst, s_sem, r_sem, me_t, me_b):
        self.a = (src, dst, s_sem, r_sem, me_t, me_b)

    def copy(self, o):
        src, dst, s_sem, r_sem, me_t, me_b = self.a
        peer = lax.rem(me_b + o, NB)
        return pltpu.make_async_remote_copy(
            src_ref=src.at[peer],
            dst_ref=dst.at[me_b],
            send_sem=s_sem,
            recv_sem=r_sem,
            device_id=(me_t, peer),
            device_id_type=MESH,
        )

    def start(self):
        def one(o, c):
            self.copy(o).start()
            return c

        lax.fori_loop(1, NB, one, 0)

    def all(self):
        src, dst, s_sem, r_sem, me_t, me_b = self.a
        rest = pl.ds(0, NB - 1)
        return pltpu.make_async_remote_copy(
            src_ref=src.at[rest],
            dst_ref=dst.at[rest],
            send_sem=s_sem,
            recv_sem=r_sem,
            device_id=(me_t, lax.rem(me_b + 1, NB)),
            device_id_type=MESH,
        )

    def wait_recv(self):
        self.all().wait_recv()

    def wait_send(self):
        self.all().wait_send()


class Face:
    def __init__(self, src, dst, s_sem, r_sem, me_t, me_b):
        self.a = (src, dst, s_sem, r_sem, me_t, me_b)

    def copy(self, side, arrival=False):
        src, dst, s_sem, r_sem, me_t, me_b = self.a
        at = side if arrival else 1 - side
        return pltpu.make_async_remote_copy(
            src_ref=src.at[side],
            dst_ref=dst.at[at],
            send_sem=s_sem.at[side],
            recv_sem=r_sem.at[at],
            device_id=(me_t + (1 if side else -1), me_b),
            device_id_type=MESH,
        )

    def there(self, side):
        return (self.a[4] < 3) if side else (self.a[4] > 0)

    def start(self):
        for side in range(2):

            @pl.when(self.there(side))
            def _(side=side):
                self.copy(side).start()

    def wait(self):
        for side in range(2):

            @pl.when(self.there(side))
            def _(side=side):
                self.copy(side, True).wait_recv()
                self.copy(side).wait_send()


def split(x):
    high = x.astype(bf16).astype(f32)
    return high, x - high


def ahead(v, k):
    return pltpu.roll(v, NV - k, 1)


def prepare(xs, vs, stiff, lx, lc, ab):
    one = jnp.ones((8, NV), f32)
    zero = jnp.zeros((8, NV), f32)
    cs = [(v + ahead(v, 1) + ahead(v, 2)) * (1.0 / 3.0) for v in vs]
    xp = [x * SQ for x in xs]
    cp = [c * SQ for c in cs]
    x1, x2 = zip(*[split(x) for x in xp])
    c1, c2 = zip(*[split(c) for c in cp])
    n = -0.5 * (xp[0] * xp[0] + xp[1] * xp[1] + xp[2] * xp[2])
    m = -0.5 * (cp[0] * cp[0] + cp[1] * cp[1] + cp[2] * cp[2]) + jnp.log2(stiff) - 7.0
    n1, r = split(n)
    n2, n3 = split(r)
    m1, r = split(m)
    m2, m3 = split(r)
    for k, r in enumerate([*x1, *x1, *x2, n1, n2, n3, one, one, one, zero]):
        ab[0, 8 * k : 8 * k + 8, :] = r
    for k, r in enumerate([*c1, *c2, *c1, one, one, one, m1, m2, m3, zero]):
        ab[1, 8 * k : 8 * k + 8, :] = r
    for ref, rows in ((lx, [*x1, *x2, one, zero]), (lc, [*c1, *c2, one, zero])):
        for k, r in enumerate(rows):
            ref[pl.ds(k, 8, stride=8), :] = r
    return cs


def energies(ab, t):
    def get(side, p):
        return ab[side, pl.ds(p, 16, stride=8), :].astype(bf16)

    cat = jnp.concatenate
    a = cat([get(0, 2 * t), get(0, 2 * t + 1)], 0).T
    b0 = get(1, 2 * t)
    b1 = get(1, 2 * t + 1)
    zero = jnp.zeros_like(b0)
    b = cat([cat([b0, zero], 1), cat([zero, b1], 1)], 0)
    e = jnp.exp2(jnp.dot(a, b, preferred_element_type=f32))
    high = e.astype(bf16)
    return high, (e - high.astype(f32)).astype(bf16)


def sums(t, e, lx, lc, rx, rc):
    h0, l0, h1, l1 = e
    rows = slice(16 * t, 16 * t + 16)
    x = lx[rows, :].astype(bf16)
    c = lc[rows, :].astype(bf16)
    cat = jnp.concatenate
    e_ij = cat([cat([h0, h1], 1), cat([l0, l1], 1)], 0)
    e_ji = cat([cat([h0, l0], 1), cat([h1, l1], 1)], 0)
    r = jnp.dot(cat([x, x], 1), e_ij, preferred_element_type=f32)
    s = lax.dot_general(cat([c, c], 1), e_ji, DN, preferred_element_type=f32)
    for ref, v in ((rx, r), (rc, s)):
        ref[16 * t : 16 * t + 8, :] = v[0:8, 0:NV]
        ref[16 * t + 8 : 16 * t + 16, :] = v[8:16, NV : 2 * NV]


def forces(xs, cs, rx, rc):
    def get(ref, k):
        return ref[pl.ds(k, 8, stride=8), :]

    inv = 1.0 / SQ
    q = get(rx, 6)
    r = get(rc, 6)
    react = [cs[k] * q - (get(rx, k) + get(rx, 3 + k)) * inv for k in range(3)]
    push = [xs[k] * r - (get(rc, k) + get(rc, 3 + k)) * inv for k in range(3)]
    return push, react


class Groups:
    def __init__(self, xg, vg, sg, lx, lc, rx, rc, eb, ab):
        self.r = (xg, vg, sg, lx, lc, rx, rc, eb, ab)

    def second(self, i, g, put):
        xg, vg, sg, lx, lc, rx, rc, eb, ab = self.r
        u, t = divmod(i, 4)
        e = [eb[u, t, k] for k in range(4)]
        sums(t, e, lx.at[u], lc.at[u], rx.at[u], rc.at[u])
        if t == 3:
            xs = [xg[u, c] for c in range(3)]
            cs = [vg[u, c] for c in range(3)]
            put(g, *forces(xs, cs, rx.at[u], rc.at[u]))

    def phase(self, base, count, load, put, before=None):
        xg, vg, sg, lx, lc, rx, rc, eb, ab = self.r
        for i in range(count * 4):
            u, t = divmod(i, 4)
            if t == 0:
                load(u, base + u)
                xs = [xg[u, c] for c in range(3)]
                vs = [vg[u, c] for c in range(3)]
                cs = prepare(xs, vs, sg[u], lx.at[u], lc.at[u], ab.at[u])
                for c in range(3):
                    vg[u, c] = cs[c]
            j = i - LAG
            if j >= 0:
                self.second(j, base + j // 4, put)
            elif before is not None:
                n, last, put_last = before
                self.second(n * 4 + j, last, put_last)
            high, low = energies(ab.at[u], t)
            eb[u, t, 0] = high[:, :NV]
            eb[u, t, 1] = low[:, :NV]
            eb[u, t, 2] = high[:, NV:]
            eb[u, t, 3] = low[:, NV:]
        return count, base + count - 1, put

    def flush(self, before):
        n, last, put = before
        for j in range(n * 4 - LAG, n * 4):
            self.second(j, last, put)

    def loop(self, total, count, load, put, after):
        def step(s, carry):
            base = s * count
            self.phase(base, count, load, put, (count, jnp.maximum(base - 1, 0), put))
            for u in range(count):
                after(base + u - 1)
            return carry

        lax.fori_loop(0, total // count, step, 0)
        self.flush((count, total - 1, put))
        after(total - 1)


def rows8(g):
    return pl.ds(pl.multiple_of(g * 8, 8), 8)


def pair_kernel(
    *refs,
):
    ins, refs = refs[:8], refs[8:]
    outs, refs = refs[:5], refs[5:]
    ret_b, ret_f, *refs = refs
    here, refs = refs[:8], refs[8:]
    rp, fp, loc, pick, fpick, rs, verts, stiff = here
    made, refs = refs[:5], refs[5:]
    push_l, react_l, react_b, react_f, meta = made
    got_b, got_f, out_b, out_f, back_b, back_f, brd, gv, *work, sems, fsems, isems, osems = refs
    xg, vg, sg = work[:3]
    me_t = lax.axis_index("slab")
    me_b = lax.axis_index("brick")
    halves = [pl.ds(h * (NP // 2), NP // 2) for h in range(2)]
    moves = [(ins[6].at[c, h, :], verts.at[c, h, :]) for c in range(3) for h in halves]
    moves += [(ins[7].at[h, :], stiff.at[h, :]) for h in halves]
    moves += list(zip(ins[:6], here[:6]))
    moves = [pltpu.make_async_copy(a, b, isems.at[k]) for k, (a, b) in enumerate(moves)]
    for move in moves:
        move.start()
    barrier = greet(me_t, me_b)
    for move in moves:
        move.wait()
    ask_b = Brick(out_b, got_b, sems.at[0], sems.at[1], me_t, me_b)
    ask_f = Face(out_f, got_f, fsems.at[0], fsems.at[1], me_t, me_b)
    give_b = Brick(back_b, ret_b, sems.at[2], sems.at[3], me_t, me_b)
    give_f = Face(back_f, ret_f, fsems.at[2], fsems.at[3], me_t, me_b)

    def row(c, idx):
        return jnp.where(idx >= 0, verts[c, pl.ds(jnp.maximum(idx, 0), 1), :], FAR)

    for s in range(NB):
        out_b[s, 3] = jnp.broadcast_to(rs[:, s : s + 1].astype(f32), (NS, NV))
    got_b[me_b, 0:3] = jnp.full((3, NS, NV), FAR, f32)
    got_b[me_b, 3] = jnp.zeros((NS, NV), f32)

    @pl.when(me_t == 0)
    def _():
        got_f[0] = jnp.full((3, NF, NV), FAR, f32)

    @pl.when(me_t == 3)
    def _():
        got_f[1] = jnp.full((3, NF, NV), FAR, f32)

    groups = Groups(*work)
    half = NF // 8

    def pushing(u, p, idx):
        for c in range(3):
            vg[u, c, p : p + 1, :] = verts[c, pl.ds(idx, 1), :]
        sg[u, p : p + 1, :] = stiff[pl.ds(idx, 1), :]

    def load_local(u, g):
        for p in range(8):
            a = loc[0, g * 8 + p]
            for c in range(3):
                xg[u, c, p : p + 1, :] = verts[c, pl.ds(a, 1), :]
            pushing(u, p, loc[1, g * 8 + p])

    def load_first(u, g):
        load_local(u, g)
        for h in range(2):
            s = 2 * g + h
            for k in range(NS):
                for c in range(3):
                    out_b[s, c, k : k + 1, :] = row(c, rp[k, s])
        side = g // half
        for k in range(8):
            j = lax.rem(g, half) * 8 + k
            for c in range(3):
                out_f[side, c, pl.ds(j, 1), :] = row(c, fp[side, j])

    def put_local(g, push, re):
        for c in range(3):
            push_l[c, rows8(g), :] = push[c]
            react_l[c, rows8(g), :] = re[c]

    tail = groups.phase(0, FIRST, load_first, put_local)
    greeted(barrier, me_t)
    ask_f.start()
    ask_b.start()
    tail = groups.phase(FIRST, SECOND, load_local, put_local, tail)
    copies = []

    def give_out(k, rows=None, slot=None):
        a, b = made[k], outs[k]
        if rows is not None:
            a, b = a.at[:, rows, :], b.at[:, rows, :]
        copies.append(pltpu.make_async_copy(a, b, osems.at[k if slot is None else slot]))
        copies[-1].start()

    cut = 8 * (FIRST + SECOND)
    early = pl.ds(0, cut)
    rest = pl.ds(cut, NL - cut)

    def load_face(u, g):
        side = g // half
        k = lax.rem(g, half)
        for c in range(3):
            xg[u, c] = got_f[side, c, rows8(k), :]
        for p in range(8):
            pushing(u, p, fpick[side, k * 8 + p])
            j = g * 8 + p
            idx = pick[0, j]
            for c in range(3):
                brd[c, pl.ds(j, 1), :] = verts[c, pl.ds(idx, 1), :]
            brd[3, pl.ds(j, 1), :] = stiff[pl.ds(idx, 1), :]

    def put_face(g, push, re):
        side = g // half
        k = lax.rem(g, half)
        for c in range(3):
            back_f[side, c, rows8(k), :] = push[c]
            react_f[c, rows8(g), :] = re[c]

    ask_f.wait()
    groups.flush(groups.phase(0, 2 * half, load_face, put_face, tail))
    give_f.start()
    give_out(3)
    give_out(0, early)
    give_out(1, early)
    ends = [pltpu.make_async_copy(back_f.at[k], ret_f.at[k], fsems.at[4, k]) for k in range(2)]
    for side in range(2):

        @pl.when(jnp.logical_not(give_f.there(side)))
        def _(side=side):
            ends[side].start()

    ask_b.wait_recv()
    table = jnp.concatenate([brd[c] for c in range(4)], 1)
    t1 = table.astype(bf16)
    r = table - t1.astype(f32)
    t2 = r.astype(bf16)
    t3 = (r - t2.astype(f32)).astype(bf16)
    parts = jnp.concatenate([t1, t2, t3], 0)
    lane = lax.broadcasted_iota(i32, (NV, NV), 1).astype(f32)
    for h in range(NBS // NV):
        want = jnp.concatenate([got_b[h * 16 + s, 3] for s in range(16)], 0)
        for s in range(16):
            meta[h * 16 + s] = got_b[h * 16 + s, 3]
        hot = jnp.where(want == lane, 1.0, 0.0).astype(bf16)
        v = jnp.dot(jnp.concatenate([hot] * 3, 1), parts, preferred_element_type=f32)
        for c in range(4):
            gv[c, h * NV : (h + 1) * NV, :] = v[:, c * NV : (c + 1) * NV]

    give_out(4)

    def load_brick(u, o):
        s = lax.rem(me_b + o, NB)
        for c in range(3):
            xg[u, c] = got_b[s, c]
            vg[u, c] = gv[c, rows8(s), :]
        sg[u] = gv[3, rows8(s), :]

    def put_brick(o, push, re):
        s = lax.rem(me_b + o, NB)
        for c in range(3):
            back_b[s, c] = push[c]
            react_b[c, rows8(s), :] = re[c]

    def send_back(o):
        @pl.when(o >= 1)
        def _():
            give_b.copy(o).start()

    groups.loop(NB, U, load_brick, put_brick, send_back)
    give_out(2)
    own = pltpu.make_async_copy(back_b.at[me_b], ret_b.at[me_b], osems.at[5])
    own.start()
    late = FIRST + SECOND
    groups.flush(groups.phase(late, NL // 8 - late, load_local, put_local))
    give_out(0, rest, 6)
    give_out(1, rest, 7)
    ask_b.wait_send()
    give_b.wait_recv()
    give_b.wait_send()
    give_f.wait()
    for side in range(2):

        @pl.when(jnp.logical_not(give_f.there(side)))
        def _(side=side):
            ends[side].wait()

    own.wait()
    for copy in copies:
        copy.wait()


MADE = ((3, NL, NV), (3, NL, NV), (3, NBS, NV), (3, 2 * NF, NV), (NB, NS, NV))
BACK = ((NB, 3, NS, NV), (2, 3, NF, NV))


def pairs(rp, fp, loc, pick, fpick, rs, verts, stiff):
    sds = jax.ShapeDtypeStruct
    return pl.pallas_call(
        pair_kernel,
        name="pairs",
        out_shape=tuple(sds(shape, f32) for shape in MADE + BACK),
        in_specs=[hbm] * 8,
        out_specs=(hbm,) * 7,
        scratch_shapes=[
            *[pltpu.SMEM(shape, i32) for shape in LISTS],
            pltpu.VMEM((NS, NB), i32),
            pltpu.VMEM((3, NP, NV), f32),
            pltpu.VMEM((NP, NV), f32),
            *[pltpu.VMEM(shape, f32) for shape in MADE],
            pltpu.VMEM((NB, 4, NS, NV), f32),
            pltpu.VMEM((2, 3, NF, NV), f32),
            pltpu.VMEM((NB, 4, NS, NV), f32),
            pltpu.VMEM((2, 3, NF, NV), f32),
            pltpu.VMEM((NB, 3, NS, NV), f32),
            pltpu.VMEM((2, 3, NF, NV), f32),
            pltpu.VMEM((4, NV, NV), f32),
            pltpu.VMEM((4, NBS, NV), f32),
            pltpu.VMEM((U, 3, 8, NV), f32),
            pltpu.VMEM((U, 3, 8, NV), f32),
            pltpu.VMEM((U, 8, NV), f32),
            *[pltpu.VMEM((U, 64, NV), f32)] * 4,
            pltpu.VMEM((U, 4, 4, NV, NV), bf16),
            pltpu.VMEM((U, 2, NV, NV), f32),
            pltpu.SemaphoreType.DMA((4,)),
            pltpu.SemaphoreType.DMA((5, 2)),
            pltpu.SemaphoreType.DMA((14,)),
            pltpu.SemaphoreType.DMA((8,)),
        ],
        compiler_params=pltpu.CompilerParams(collective_id=0, has_side_effects=True),
    )(rp, fp, loc, pick, fpick, rs, verts, stiff)


def flat(a):
    lane = lax.broadcasted_iota(i32, (NB, NBS), 1)
    wide = (lane // NS == lax.broadcasted_iota(i32, (NB, NBS), 0)).astype(f32).astype(bf16)
    high, low = split(a.astype(f32))
    row = jnp.dot(high.astype(bf16), wide, preferred_element_type=f32)
    row = row + jnp.dot(low.astype(bf16), wide, preferred_element_type=f32)
    own = lax.broadcasted_iota(i32, (NS, NBS), 0) == lax.broadcasted_iota(i32, (NS, NBS), 1) % NS
    return jnp.sum(jnp.where(own, row, 0.0), axis=0, keepdims=True)


def two(x):
    high, low = split(x)
    return high.astype(bf16), low.astype(bf16)


def side_by_side(a):
    return jnp.concatenate([a[0:1], a[1:2]], 1).astype(f32)


def merge_kernel(*refs):
    n_in = 5 + len(MADE) + len(BACK)
    ins, out, here, refs = refs[:n_in], refs[n_in], refs[n_in + 1 : 2 * n_in + 1], refs[2 * n_in + 1 :]
    rp, fp, loc, pick, fpick, push_l, react_l, react_b, react_f, meta, ret_b, ret_f = here
    made, isems, osems = refs
    moves = [pltpu.make_async_copy(a, b, isems.at[k]) for k, (a, b) in enumerate(zip(ins, here))]
    order = [9, 7, 0, 1, 2, 3, 4, 5, 6, 8, 10, 11]
    for k in order:
        moves[k].start()
    for k in order[:2]:
        moves[k].wait()
    cat = jnp.concatenate

    def lanes(ref):
        return cat([ref[c] for c in range(3)], 1)

    lane = lax.broadcasted_iota(i32, (NV, NV), 1).astype(f32)
    hots = []
    for h in range(NBS // NV):
        want = cat([meta[h * 16 + s] for s in range(16)], 0)
        hots.append(jnp.where(want == lane, 1.0, 0.0).astype(bf16))
    hot = cat(hots, 0)
    border = lax.dot_general(cat([hot] * 2, 0), cat(two(lanes(react_b)), 0), D0, preferred_element_type=f32)
    for k in order[2:7]:
        moves[k].wait()
    pushed = cat([loc[0:1].astype(f32), flat(rp[...]), side_by_side(fp[...])], 1)
    pushing = cat([loc[1:2].astype(f32), pick[...].astype(f32), side_by_side(fpick[...])], 1)
    for k in order[7:]:
        moves[k].wait()

    back_b = cat([cat([ret_b[s, c] for s in range(NB)], 0) for c in range(3)], 1)
    back_f = cat([cat([ret_f[k, c] for k in range(2)], 0) for c in range(3)], 1)
    push = cat(two(cat([lanes(push_l), back_b, back_f], 0)), 0)
    react = cat(two(cat([lanes(react_l), border, lanes(react_f)], 0)), 0)

    size = NP // CHUNKS
    copies = []
    for n in range(CHUNKS):

        def scatter(idx, values):
            row = lax.broadcasted_iota(i32, (size, idx.shape[1]), 0).astype(f32) + float(n * size)
            one = jnp.where(row == idx, 1.0, 0.0).astype(bf16)
            return jnp.dot(cat([one, one], 1), values, preferred_element_type=f32)

        p = scatter(pushed, push)
        q = scatter(pushing, react)
        rows = pl.ds(n * size, size)
        for c in range(3):
            r = q[:, c * NV : (c + 1) * NV]
            s = r + pltpu.roll(r, 1, 1) + pltpu.roll(r, 2, 1)
            made[c, rows, :] = p[:, c * NV : (c + 1) * NV] + s * (1.0 / 3.0)
        copies.append(pltpu.make_async_copy(made.at[:, rows, :], out.at[:, rows, :], osems.at[n]))
        copies[-1].start()
    for copy in copies:
        copy.wait()


def merge(*args):
    return pl.pallas_call(
        merge_kernel,
        name="merge",
        out_shape=jax.ShapeDtypeStruct((3, NP, NV), f32),
        in_specs=[hbm] * len(args),
        out_specs=hbm,
        scratch_shapes=[
            *[pltpu.VMEM(shape, i32) for shape in LISTS],
            *[pltpu.VMEM(shape, f32) for shape in MADE + BACK],
            pltpu.VMEM((3, NP, NV), f32),
            pltpu.SemaphoreType.DMA((len(args),)),
            pltpu.SemaphoreType.DMA((CHUNKS,)),
        ],
    )(*args)


def body(verts, stiffness, local_pairs, border_pick, recv_src, recv_pair, face_pick, face_pair):
    rp = recv_pair[0].T
    lists = (rp, face_pair[0], local_pairs[0], border_pick, face_pick[0])
    made = pairs(*lists, recv_src[0].T, verts.transpose(1, 0, 2), stiffness)
    return merge(*lists, *made).transpose(1, 0, 2)


def solution(mesh):
    both = ("slab", "brick")
    placed = (
        P(both, None, None),
        P(both, None),
        P(both, None, None),
        P(both, None),
        P(both, None, None),
        P(both, None, None),
        P(both, None, None),
        P(both, None, None),
    )
    return jax.shard_map(
        body, mesh=mesh, in_specs=placed, out_specs=P(both, None, None), check_vma=False
    )
```
